256 devices in a mesh: kx: 8 (over z), ht: 8 (over y, core), real: 4 (over x).
Axes of the slice: x: 4, y: 4, z: 8, core: 2. Of those that a mesh axis runs over, the one named last changes fastest.
Arguments:
- velocity: float32 [3, 4, 32, 512, 128], P(None, 'real', 'kx', 'ht'), may hold values from -6 to 6
- low_index: int32 [8], replicated, may hold values from 0 to 31, as said below
- neighbours: int32 [32, 8], P('kx'), may hold values from 0 to 31, as said below
- owner_map: int32 [64], replicated, may hold values from 0 to 63, each once
- mode_counts: int32 [32], P('kx'), may hold values from 16 to 64
- helmholtz: float32 [64, 512, 512], P(('kx', 'ht')), may hold values from -0.25 to 0.25
Outputs:
- velocity_next: float32 [3, 4, 32, 512, 128], P(None, 'real', 'kx', 'ht')
The draws below stay inside these ranges and needn't reach their ends.
Inputs may be any that keep to these rules, and one draw needn't show every extreme that they name: `low_index`: distinct values. neighbours[m, j] lies within 4 modes of m, counting circularly over the 32 modes; offsets of + 4 and - 4 both occur.
All inputs are finite; a program needn't handle non-finite values.
Results may differ from the reference program's by a relative error of at most 0.0001.
Values sent between devices are 32-bit elements; how exact they have to be, the bound alone decides.
A program may use at most 64 MiB of HBM per device.

```python
import jax
import jax.numpy as jnp
from jax import lax

COMP = 3
REALS = 4
KX_DEV = 4
KX = 32
NLOW = 8
KZ = 64
NZP = 256
NY = 512
SUBSTEPS = 1


def draw_low_index(key, part):
    return jax.random.permutation(key, KX)[:NLOW].astype(jnp.int32)


def draw_neighbours(key, part):
    offsets = jax.random.randint(jax.random.fold_in(key, 1), (KX * NLOW,), -KX_DEV, KX_DEV + 1)
    first_pick = jax.random.randint(jax.random.fold_in(key, 2), (), 0, KX * NLOW)
    second_pick = (first_pick + 1 + jax.random.randint(jax.random.fold_in(key, 3), (), 0, KX * NLOW - 1)) % (KX * NLOW)
    flat_offsets = offsets.at[first_pick].set(KX_DEV).at[second_pick].set(-KX_DEV)
    return ((jnp.arange(KX)[:, None] + flat_offsets.reshape(KX, NLOW)) % KX).astype(jnp.int32)


def set_ends(drawn, own_key, smallest, largest):
    place = [jax.random.randint(jax.random.fold_in(own_key, axis), (), 0, length) for axis, length in enumerate(drawn.shape)]
    main_axis = drawn.shape.index(max(drawn.shape))
    next_to = place[:main_axis] + [(place[main_axis] + 1) % drawn.shape[main_axis]] + place[main_axis + 1:]
    return drawn.at[tuple(place)].set(smallest).at[tuple(next_to)].set(largest)


def shard_levels(own_key, extent, pieces, low, largest):
    def one(position, shards_of):
        steps = jax.random.uniform(jax.random.fold_in(jax.random.fold_in(own_key, 6), position), (shards_of,), jnp.float32, low / len(pieces), largest / len(pieces))
        return jnp.repeat(jnp.exp(steps), extent[position] // shards_of).reshape((-1,) + (1,) * (len(extent) - position - 1))

    gain = one(*pieces[0])
    for cut in pieces[1:]:
        gain = gain * one(*cut)
    return gain


def noise(rng, shape, spread, most, pieces=(), held_as=jnp.bfloat16):
    gain = shard_levels(rng, shape, pieces, -0.22, 0.18) if pieces else 1.0
    drawn = jax.random.normal(rng, shape, jnp.float32) * spread * gain
    return jnp.minimum(jnp.maximum(drawn, -most), most).astype(held_as)


def setup_inputs(seed: int = 0) -> dict:
    streams_of = jax.random.split(jax.random.key(seed), 7)
    return {
        "velocity": noise(streams_of[0], (COMP, REALS, KX, NY, 2 * KZ), 1.0, 6.0, ((1, 4), (2, 8), (3, 8)), jnp.float32),
        "low_index": draw_low_index(jax.random.fold_in(streams_of[6], 71), 0),
        "neighbours": draw_neighbours(jax.random.fold_in(streams_of[6], 71), 0),
        "owner_map": jax.random.permutation(streams_of[3], KZ).astype(jnp.int32),
        "mode_counts": set_ends(jax.random.randint(streams_of[4], (KX,), KZ // 4, KZ + 1), jax.random.fold_in(streams_of[4], 1), KZ // 4, KZ).astype(jnp.int32),
        "helmholtz": noise(streams_of[5], (KZ, NY, NY), NY ** -0.5, 0.25, ((0, 64),), jnp.float32),
    }


dt_step = 0.1

def spanwise_tables(mode_count, point_count):
    column_ids = jnp.arange(2 * mode_count)
    wavenumber = (column_ids // 2).astype(jnp.float32)
    imag_part = column_ids % 2
    positions = 2.0 * jnp.pi * jnp.arange(point_count).astype(jnp.float32) / point_count
    phases = wavenumber[:, None] * positions[None, :]
    forward = jnp.where(imag_part[:, None] == 0, jnp.cos(phases), -jnp.sin(phases)) / jnp.sqrt(jnp.float32(mode_count))
    backward = forward.T * (2.0 * mode_count / point_count)
    return (forward, backward)

def reference(velocity, low_index, neighbours, owner_map, mode_counts, helmholtz):
    highest = lax.Precision.HIGHEST
    forward, backward = spanwise_tables(KZ, NZP)
    kx_modes = jnp.arange(KX, dtype=jnp.int32)
    low_select = (low_index[:, None] == kx_modes[None, :]).astype(jnp.float32)
    high_mask = 1.0 - lax.optimization_barrier(jnp.sum(low_select, axis=0))
    column_mask = ((jnp.arange(2 * KZ) // 2)[None, :] < mode_counts[:, None]).astype(jnp.float32)
    inverse_map = jnp.zeros((KZ,), jnp.int32).at[owner_map].set(jnp.arange(KZ, dtype=jnp.int32))
    current = velocity

    def one_real(fields):
        physical = jnp.dot(fields, forward, precision=highest)
        low_fields = jnp.einsum('jm,cmyz->cjyz', low_select, physical, precision=highest)
        high_low = jnp.zeros_like(physical)
        stresses = []
        for member in range(NLOW):
            partner = jnp.take(physical, neighbours[:, member], axis=1)
            low_one = low_fields[:, member:member + 1]
            high_low = high_low + low_one * partner[1:2] + partner * low_one[1:2]
            weighted = physical * (partner[1:2] * high_mask[None, :, None, None])
            stresses.append(lax.optimization_barrier(jnp.sum(weighted, axis=1)))
        return (jnp.dot(high_low, backward, precision=highest), jnp.stack(stresses, axis=1))
    for substep in range(SUBSTEPS):
        nonlinear, stress = lax.map(one_real, jnp.moveaxis(current, 1, 0))
        nonlinear = jnp.moveaxis(nonlinear, 0, 1)
        low_forcing = jnp.dot(lax.optimization_barrier(jnp.sum(stress, axis=0)) / REALS, backward, precision=highest)
        forcing = nonlinear * high_mask[None, None, :, None, None]
        forcing = forcing + jnp.einsum('jm,cjyk->cmyk', low_select, low_forcing, precision=highest)[:, None]
        forcing = forcing * column_mask[None, None, :, None, :]
        updated = current + dt_step * forcing
        slotted = jnp.take(updated.reshape(COMP, REALS, KX, NY, KZ, 2), owner_map, axis=4)
        solved = jnp.einsum('syx,crmxsp->crmysp', helmholtz, slotted, precision=highest)
        current = jnp.take(solved, inverse_map, axis=4).reshape(COMP, REALS, KX, NY, 2 * KZ)
    return current
```

```python
import functools

import jax
import jax.numpy as jnp
import numpy as np
from jax import lax
from jax.experimental import pallas as pl
from jax.experimental.pallas import tpu as pltpu
from jax.sharding import PartitionSpec as P

MESH = pl.DeviceIdType.MESH
F32 = jnp.float32
BF16 = jnp.bfloat16

dt_step = 0.1
COMP, BAND, ROWS, COLS = 3, 4, 64, 128
NKX, NHT, NREAL = 8, 8, 4
MODES, LOW, POINTS, HEIGHTS, SLOTS = 32, 8, 256, 512, 64
ORDER = (1, 0, 2)


def spanwise_tables():
    ids = np.arange(COLS)
    wave = (ids // 2).astype(np.float32)
    spots = np.float32(2.0 * np.pi) * np.arange(POINTS).astype(np.float32) / np.float32(POINTS)
    phases = (wave[:, None] * spots[None, :]).astype(np.float64)
    forward = np.where(ids[:, None] % 2 == 0, np.cos(phases), -np.sin(phases)) / 8.0
    forward = forward.astype(np.float32)
    backward = np.ascontiguousarray(forward.T) * np.float32(0.5)

    def halves(table):
        head = table.astype(BF16)
        return head, (table - head.astype(np.float32)).astype(BF16)

    return (*halves(forward), *halves(backward))


def split(x):
    head = x.astype(BF16)
    return head, (x - head.astype(F32)).astype(BF16)


def mm(a, b):
    return lax.dot_general(a, b, (((1,), (0,)), ((), ())), preferred_element_type=F32)


def mm_nt(a, b):
    return lax.dot_general(a, b, (((1,), (1,)), ((), ())), preferred_element_type=F32)


def mm3(x, head, tail):
    hi, lo = split(x)
    return mm(hi, head) + (mm(hi, tail) + mm(lo, head))


def kernel(
    v, low_s, nb_own, omap_s, cnt_own, helm, t_fh, t_fl, t_bh, t_bl,
    out,
    vr, phys, hl, nl, upd, snd, ubuf, wsnd, rbuf, strs, zlow, onehot, oh, oht, hf, hth, htl,
    fh, fl, bh, bl, nb_s, cnt_s, inv_s,
    a_send, a_recv, i_send, i_recv, st_send, st_recv, b_send, b_recv, c_send, c_recv, l_sem,
):
    kx, ht, re = lax.axis_index("kx"), lax.axis_index("ht"), lax.axis_index("real")
    slot = kx * NHT + ht
    source = ht * NKX + kx

    barrier = pltpu.get_barrier_semaphore()
    for d in range(1, NKX):
        pl.semaphore_signal(barrier, 1, device_id=(lax.rem(kx + d, NKX), ht, re), device_id_type=MESH)
    for d in range(1, NHT):
        pl.semaphore_signal(barrier, 1, device_id=(kx, lax.rem(ht + d, NHT), re), device_id_type=MESH)
    for d in range(1, NREAL):
        pl.semaphore_signal(barrier, 1, device_id=(kx, ht, lax.rem(re + d, NREAL)), device_id_type=MESH)

    local = [
        pltpu.make_async_copy(src, dst, l_sem.at[i])
        for i, (src, dst) in enumerate(
            ((helm.at[0], hf), (t_fh, fh), (t_fl, fl), (t_bh, bh), (t_bl, bl))
        )
    ]
    for copy in local:
        copy.start()
    for i, c in enumerate(ORDER):
        for a in range(2):
            pltpu.make_async_copy(
                v.at[c, 0, :, pl.ds(a * 32 + kx * 4, 4), :],
                vr.at[c, pl.ds(kx * BAND, BAND), pl.ds(a * 4, 4), :],
                a_recv.at[c],
            ).start()
    pltpu.make_async_copy(nb_own, nb_s.at[kx], i_recv.at[0]).start()
    pltpu.make_async_copy(cnt_own, cnt_s.at[kx], i_recv.at[1]).start()

    pl.semaphore_wait(barrier, (NKX - 1) + (NHT - 1) + (NREAL - 1))

    for d in range(1, NKX):
        peer = lax.rem(kx + d, NKX)
        for own, table, i in ((nb_own, nb_s, 0), (cnt_own, cnt_s, 1)):
            pltpu.make_async_remote_copy(
                own, table.at[kx], i_send.at[i], i_recv.at[i], device_id=(peer, ht, re), device_id_type=MESH
            ).start()
    for c in ORDER:
        for d in (4, 3, 5, 2, 6, 1, 7):
            peer = lax.rem(kx + d, NKX)
            for a in range(2):
                pltpu.make_async_remote_copy(
                    v.at[c, 0, :, pl.ds(a * 32 + peer * 4, 4), :],
                    vr.at[c, pl.ds(kx * BAND, BAND), pl.ds(a * 4, 4), :],
                    a_send.at[c],
                    a_recv.at[c],
                    device_id=(peer, ht, re),
                    device_id_type=MESH,
                ).start()

    lane = lax.broadcasted_iota(jnp.int32, (1, COLS), 1)

    def one_row(s, _):
        for p in range(2):
            onehot[pl.ds(p * SLOTS + s, 1), :] = (lane == 2 * omap_s[s] + p).astype(F32)
        return 0

    lax.fori_loop(0, SLOTS, one_row, 0)
    square = onehot[...]
    oh[...] = square.astype(BF16)
    oht[...] = square.T.astype(BF16)

    def one_mode(m, _):
        place = jnp.int32(LOW)
        for j in range(LOW):
            place = jnp.where(low_s[j] == m, jnp.int32(j), place)
        inv_s[m] = place
        return 0

    lax.fori_loop(0, MODES, one_mode, 0)
    for c in range(COMP):
        zlow[c, LOW] = jnp.zeros((8, COLS), F32)
    for copy in local:
        copy.wait()
    for i in range(4):
        for j in range(4):
            block = hf[pl.ds(i * 128, 128), pl.ds(j * 128, 128)].T
            head, tail = split(block)
            hth[pl.ds(j * 128, 128), pl.ds(i * 128, 128)] = head
            htl[pl.ds(j * 128, 128), pl.ds(i * 128, 128)] = tail
    pltpu.make_async_copy(nb_s, nb_s, i_recv.at[0]).wait()
    pltpu.make_async_copy(cnt_s, cnt_s, i_recv.at[1]).wait()

    def products(c):
        pltpu.make_async_copy(vr.at[c], vr.at[c], a_recv.at[c]).wait()
        fields = vr[c].reshape(MODES * 8, COLS)
        phys[c] = mm3(fields, fh[...], fl[...]).reshape(MODES, 8, POINTS)
        sums = []
        for half in range(2):
            part = pl.ds(half * 128, 128)
            low_1 = [phys[1, low_s[j], :, part] for j in range(LOW)]
            low_c = low_1 if c == 1 else [phys[c, low_s[j], :, part] for j in range(LOW)]

            def one(m, sums, part=part, low_1=low_1, low_c=low_c):
                high = (inv_s[m] == LOW).astype(F32)
                mine = phys[c, m, :, part] * high
                band, row = m // BAND, lax.rem(m, BAND)
                total = jnp.zeros((8, 128), F32)
                new = []
                for j in range(LOW):
                    near = nb_s[band, row, j]
                    p_1 = phys[1, near, :, part]
                    if c == 1:
                        total = total + low_1[j] * p_1
                    else:
                        total = total + (low_c[j] * p_1 + phys[c, near, :, part] * low_1[j])
                    new.append(sums[j] + mine * p_1)
                if c == 1:
                    total = total + total
                hl[m, :, part] = total * high
                return tuple(new)

            sums.append(lax.fori_loop(0, MODES, one, tuple(jnp.zeros((8, 128), F32) for _ in range(LOW))))
        stress = jnp.concatenate(
            [jnp.concatenate([sums[0][j], sums[1][j]], axis=1) for j in range(LOW)], axis=0
        )
        strs[re, c] = mm3(stress * (1.0 / NREAL), bh[...], bl[...])
        for d in range(1, NREAL):
            pltpu.make_async_remote_copy(
                strs.at[re, c],
                strs.at[re, c],
                st_send.at[c],
                st_recv.at[c],
                device_id=(kx, ht, lax.rem(re + d, NREAL)),
                device_id_type=MESH,
            ).start()
        nl[c] = mm3(hl[...].reshape(MODES * 8, POINTS), bh[...], bl[...]).reshape(MODES, 8, COLS)

    def forced(c):
        pltpu.make_async_copy(strs.at[pl.ds(0, 3), 0], strs.at[pl.ds(0, 3), 0], st_recv.at[c]).wait()
        summed = (strs[0, c] + strs[1, c]) + (strs[2, c] + strs[3, c])
        zlow[c, pl.ds(0, LOW)] = summed.reshape(LOW, 8, COLS)
        half_lane = lax.broadcasted_iota(jnp.int32, (8, COLS), 1) // 2

        def one(m, _):
            gain = jnp.where(half_lane < cnt_s[m // BAND, lax.rem(m, BAND)], F32(dt_step), F32(0.0))
            upd[pl.ds(m * 8, 8), :] = vr[c, m] + gain * (nl[c, m] + zlow[c, inv_s[m]])
            return 0

        lax.fori_loop(0, MODES, one, 0)
        rows = [
            upd[pl.ds(a * 4 + 2 * tile + y, MODES, stride=8), :]
            for tile in range(2)
            for a in range(2)
            for y in range(2)
        ]
        hi, lo = split(jnp.concatenate(rows, axis=0))
        turned = mm_nt(oh[...], hi) + mm_nt(oh[...], lo)
        odd = (lax.broadcasted_iota(jnp.int32, (SLOTS, 128), 1) // 32) % 2 == 1
        for tile in range(2):
            even_p = turned[:SLOTS, tile * 128 : tile * 128 + 128]
            odd_p = turned[SLOTS:, tile * 128 : tile * 128 + 128]
            first = jnp.where(odd, pltpu.roll(odd_p, 32, 1), even_p)
            second = jnp.where(odd, odd_p, pltpu.roll(even_p, 96, 1))
            snd[c, pl.ds(2 * tile, SLOTS, stride=4), :] = first
            snd[c, pl.ds(2 * tile + 1, SLOTS, stride=4), :] = second
        pltpu.make_async_copy(
            snd.at[c, pl.ds(slot * 4, 4), :], ubuf.at[c, pl.ds(source * 4, 4), :], b_recv.at[c]
        ).start()

        def send(t, _):
            to_kx, to_ht = lax.rem(kx + lax.rem(t, NKX), NKX), lax.rem(ht + t // NKX, NHT)
            pltpu.make_async_remote_copy(
                snd.at[c, pl.ds((to_kx * NHT + to_ht) * 4, 4), :],
                ubuf.at[c, pl.ds(source * 4, 4), :],
                b_send.at[c],
                b_recv.at[c],
                device_id=(to_kx, to_ht, re),
                device_id_type=MESH,
            ).start()
            return 0

        lax.fori_loop(1, SLOTS, send, 0)

    first_half = lax.broadcasted_iota(jnp.int32, (MODES, 128), 1) < 64

    def solved(c):
        pltpu.make_async_copy(ubuf.at[c], ubuf.at[c], b_recv.at[c]).wait()
        given = ubuf[c]
        swapped = pltpu.roll(given, 64, 1)
        pieces = []
        for block in range(NHT):
            pieces += [given[block * 32 : block * 32 + 32], swapped[block * 32 : block * 32 + 32]]
        fields = jnp.concatenate(pieces, axis=0).T[:64]
        answer = mm3(fields, hth[...], htl[...])
        for tile in range(4):
            even_p = answer[:MODES, tile * 128 : tile * 128 + 128]
            odd_p = answer[MODES:, tile * 128 : tile * 128 + 128]
            wsnd[c, pl.ds((2 * tile) * MODES, MODES), :] = jnp.where(
                first_half, even_p, pltpu.roll(odd_p, 64, 1)
            )
            wsnd[c, pl.ds((2 * tile + 1) * MODES, MODES), :] = jnp.where(
                first_half, pltpu.roll(even_p, 64, 1), odd_p
            )
        pltpu.make_async_copy(
            wsnd.at[c, pl.ds(ht * MODES + kx * 4, 4), :], rbuf.at[c, pl.ds(slot * 4, 4), :], c_recv.at[c]
        ).start()

        def send(t, _):
            to_kx, to_ht = lax.rem(kx + lax.rem(t, NKX), NKX), lax.rem(ht + t // NKX, NHT)
            pltpu.make_async_remote_copy(
                wsnd.at[c, pl.ds(to_ht * MODES + to_kx * 4, 4), :],
                rbuf.at[c, pl.ds(slot * 4, 4), :],
                c_send.at[c],
                c_recv.at[c],
                device_id=(to_kx, to_ht, re),
                device_id_type=MESH,
            ).start()
            return 0

        lax.fori_loop(1, SLOTS, send, 0)

    def placed(c):
        pltpu.make_async_copy(rbuf.at[c], rbuf.at[c], c_recv.at[c]).wait()
        low_half = lax.broadcasted_iota(jnp.int32, (SLOTS, 128), 1) < 64
        columns = []
        for pair in range(2):
            one = rbuf[c, pl.ds(2 * pair, SLOTS, stride=4), :]
            two = rbuf[c, pl.ds(2 * pair + 1, SLOTS, stride=4), :]
            columns.append(
                jnp.concatenate(
                    [
                        jnp.where(low_half, one, pltpu.roll(two, 64, 1)),
                        jnp.where(low_half, pltpu.roll(one, 64, 1), two),
                    ],
                    axis=0,
                )
            )
        hi, lo = split(jnp.concatenate(columns, axis=1))
        back = mm(oht[...], hi) + mm(oht[...], lo)
        for pair in range(2):
            out[c, 0, pl.ds(2 * pair, 2), :, :] = back[:, pair * 128 : pair * 128 + 128].T.reshape(2, ROWS, COLS)

    products(1)
    products(0)
    forced(1)
    products(2)
    forced(0)
    forced(2)
    for c in ORDER:
        solved(c)
    for c in ORDER:
        placed(c)

    pltpu.make_async_copy(nb_s.at[pl.ds(0, 7)], nb_s.at[pl.ds(0, 7)], i_send.at[0]).wait()
    pltpu.make_async_copy(cnt_s.at[pl.ds(0, 7)], cnt_s.at[pl.ds(0, 7)], i_send.at[1]).wait()
    for c in range(COMP):
        sent = vr.at[c, pl.ds(0, MODES - BAND)]
        pltpu.make_async_copy(sent, sent, a_send.at[c]).wait()
        sent = strs.at[pl.ds(0, NREAL - 1), c]
        pltpu.make_async_copy(sent, sent, st_send.at[c]).wait()
        sent = snd.at[c, pl.ds(0, 252), :]
        pltpu.make_async_copy(sent, sent, b_send.at[c]).wait()
        sent = wsnd.at[c, pl.ds(0, 252), :]
        pltpu.make_async_copy(sent, sent, c_send.at[c]).wait()


def local(velocity, low_index, neighbours, owner_map, mode_counts, helmholtz):
    tables = [jnp.asarray(t) for t in spanwise_tables()]
    hbm = pl.BlockSpec(memory_space=pl.ANY)
    smem = pl.BlockSpec(memory_space=pltpu.SMEM)
    vmem = pl.BlockSpec(memory_space=pltpu.VMEM)
    dma = pltpu.SemaphoreType.DMA
    return pl.pallas_call(
        kernel,
        out_shape=jax.ShapeDtypeStruct(velocity.shape, F32),
        in_specs=[hbm, smem, hbm, smem, hbm, hbm, hbm, hbm, hbm, hbm],
        out_specs=vmem,
        scratch_shapes=[
            pltpu.VMEM((COMP, MODES, 8, COLS), F32),
            pltpu.VMEM((COMP, MODES, 8, POINTS), F32),
            pltpu.VMEM((MODES, 8, POINTS), F32),
            pltpu.VMEM((COMP, MODES, 8, COLS), F32),
            pltpu.VMEM((MODES * 8, COLS), F32),
            pltpu.VMEM((COMP, 256, 128), F32),
            pltpu.VMEM((COMP, 256, 128), F32),
            pltpu.VMEM((COMP, 256, 128), F32),
            pltpu.VMEM((COMP, 256, 128), F32),
            pltpu.VMEM((NREAL, COMP, LOW * 8, COLS), F32),
            pltpu.VMEM((COMP, LOW + 1, 8, COLS), F32),
            pltpu.VMEM((128, COLS), F32),
            pltpu.VMEM((128, COLS), BF16),
            pltpu.VMEM((COLS, 128), BF16),
            pltpu.VMEM((HEIGHTS, HEIGHTS), F32),
            pltpu.VMEM((HEIGHTS, HEIGHTS), BF16),
            pltpu.VMEM((HEIGHTS, HEIGHTS), BF16),
            pltpu.VMEM((COLS, POINTS), BF16),
            pltpu.VMEM((COLS, POINTS), BF16),
            pltpu.VMEM((POINTS, COLS), BF16),
            pltpu.VMEM((POINTS, COLS), BF16),
            pltpu.SMEM((NKX, BAND, LOW), jnp.int32),
            pltpu.SMEM((NKX, BAND), jnp.int32),
            pltpu.SMEM((MODES,), jnp.int32),
            dma((COMP,)),
            dma((COMP,)),
            dma((2,)),
            dma((2,)),
            dma((COMP,)),
            dma((COMP,)),
            dma((COMP,)),
            dma((COMP,)),
            dma((COMP,)),
            dma((COMP,)),
            dma((5,)),
        ],
        compiler_params=pltpu.CompilerParams(collective_id=0, has_side_effects=True),
    )(velocity, low_index, neighbours, owner_map, mode_counts, helmholtz, *tables)


def solution(mesh):
    in_specs = (
        P(None, "real", "kx", "ht", None),
        P(),
        P("kx", None),
        P(),
        P("kx"),
        P(("kx", "ht"), None, None),
    )
    out_specs = P(None, "real", "kx", "ht", None)
    return jax.shard_map(local, mesh=mesh, in_specs=in_specs, out_specs=out_specs, check_vma=False)
```

```python
import functools

import jax
import jax.numpy as jnp
import numpy as np
from jax import lax
from jax.experimental import pallas as pl
from jax.experimental.pallas import tpu as pltpu
from jax.sharding import PartitionSpec as P

MESH = pl.DeviceIdType.MESH
F32 = jnp.float32
BF16 = jnp.bfloat16

dt_step = 0.1
COMP, BAND, ROWS, COLS = 3, 4, 64, 128
NKX, NHT, NREAL = 8, 8, 4
MODES, LOW, POINTS, HEIGHTS, SLOTS = 32, 8, 256, 512, 64
ORDER = (1, 0, 2)


def spanwise_tables():
    ids = np.arange(COLS)
    wave = (ids // 2).astype(np.float32)
    spots = np.float32(2.0 * np.pi) * np.arange(POINTS).astype(np.float32) / np.float32(POINTS)
    phases = (wave[:, None] * spots[None, :]).astype(np.float64)
    forward = np.where(ids[:, None] % 2 == 0, np.cos(phases), -np.sin(phases)) / 8.0
    forward = forward.astype(np.float32)
    backward = np.ascontiguousarray(forward.T) * np.float32(0.5)

    def halves(table):
        head = table.astype(BF16)
        return head, (table - head.astype(np.float32)).astype(BF16)

    return (*halves(forward), *halves(backward))


def split(x):
    head = x.astype(BF16)
    return head, (x - head.astype(F32)).astype(BF16)


def mm(a, b):
    return lax.dot_general(a, b, (((1,), (0,)), ((), ())), preferred_element_type=F32)


def mm_nt(a, b):
    return lax.dot_general(a, b, (((1,), (1,)), ((), ())), preferred_element_type=F32)


def mm3(x, head, tail):
    hi, lo = split(x)
    return mm(hi, head) + (mm(hi, tail) + mm(lo, head))


def kernel(
    v, low_s, nb_own, omap_s, cnt_own, helm, t_fh, t_fl, t_bh, t_bl,
    out,
    vr, phys, hl, nl, upd, snd, ubuf, wsnd, rbuf, strs, zlow, onehot, oh, oht, hf, hth, htl,
    fh, fl, bh, bl, nb_s, cnt_s, inv_s,
    a_send, a_recv, i_send, i_recv, st_send, st_recv, b_send, b_recv, c_send, c_recv, l_sem,
):
    kx, ht, re = lax.axis_index("kx"), lax.axis_index("ht"), lax.axis_index("real")
    slot = kx * NHT + ht
    source = ht * NKX + kx
    kxs = [lax.rem(kx + d, NKX) for d in range(NKX)]
    hts = [lax.rem(ht + d, NHT) for d in range(NHT)]

    barrier = pltpu.get_barrier_semaphore()
    for d in range(1, NKX):
        pl.semaphore_signal(barrier, 1, device_id=(lax.rem(kx + d, NKX), ht, re), device_id_type=MESH)
    for d in range(1, NHT):
        pl.semaphore_signal(barrier, 1, device_id=(kx, lax.rem(ht + d, NHT), re), device_id_type=MESH)
    for d in range(1, NREAL):
        pl.semaphore_signal(barrier, 1, device_id=(kx, ht, lax.rem(re + d, NREAL)), device_id_type=MESH)

    local = [
        pltpu.make_async_copy(src, dst, l_sem.at[i])
        for i, (src, dst) in enumerate(
            ((helm.at[0], hf), (t_fh, fh), (t_fl, fl), (t_bh, bh), (t_bl, bl))
        )
    ]
    for copy in local:
        copy.start()
    for i, c in enumerate(ORDER):
        for a in range(2):
            pltpu.make_async_copy(
                v.at[c, 0, :, pl.ds(a * 32 + kx * 4, 4), :],
                vr.at[c, pl.ds(kx * BAND, BAND), pl.ds(a * 4, 4), :],
                a_recv.at[c],
            ).start()
    pltpu.make_async_copy(nb_own, nb_s.at[kx], i_recv.at[0]).start()
    pltpu.make_async_copy(cnt_own, cnt_s.at[kx], i_recv.at[1]).start()

    pl.semaphore_wait(barrier, (NKX - 1) + (NHT - 1) + (NREAL - 1))

    for d in range(1, NKX):
        peer = lax.rem(kx + d, NKX)
        for own, table, i in ((nb_own, nb_s, 0), (cnt_own, cnt_s, 1)):
            pltpu.make_async_remote_copy(
                own, table.at[kx], i_send.at[i], i_recv.at[i], device_id=(peer, ht, re), device_id_type=MESH
            ).start()
    for c in ORDER:
        for d in (4, 3, 5, 2, 6, 1, 7):
            peer = lax.rem(kx + d, NKX)
            for a in range(2):
                pltpu.make_async_remote_copy(
                    v.at[c, 0, :, pl.ds(a * 32 + peer * 4, 4), :],
                    vr.at[c, pl.ds(kx * BAND, BAND), pl.ds(a * 4, 4), :],
                    a_send.at[c],
                    a_recv.at[c],
                    device_id=(peer, ht, re),
                    device_id_type=MESH,
                ).start()

    lane = lax.broadcasted_iota(jnp.int32, (1, COLS), 1)

    def one_row(s, _):
        for p in range(2):
            onehot[pl.ds(p * SLOTS + s, 1), :] = (lane == 2 * omap_s[s] + p).astype(F32)
        return 0

    lax.fori_loop(0, SLOTS, one_row, 0)
    square = onehot[...]
    oh[...] = square.astype(BF16)
    oht[...] = square.T.astype(BF16)

    def one_mode(m, _):
        place = jnp.int32(LOW)
        for j in range(LOW):
            place = jnp.where(low_s[j] == m, jnp.int32(j), place)
        inv_s[m] = place
        return 0

    lax.fori_loop(0, MODES, one_mode, 0)
    for c in range(COMP):
        zlow[c, LOW] = jnp.zeros((8, COLS), F32)
    for copy in local:
        copy.wait()
    for i in range(4):
        for j in range(4):
            block = hf[pl.ds(i * 128, 128), pl.ds(j * 128, 128)].T
            head, tail = split(block)
            hth[pl.ds(j * 128, 128), pl.ds(i * 128, 128)] = head
            htl[pl.ds(j * 128, 128), pl.ds(i * 128, 128)] = tail
    pltpu.make_async_copy(nb_s, nb_s, i_recv.at[0]).wait()
    pltpu.make_async_copy(cnt_s, cnt_s, i_recv.at[1]).wait()

    def products(c):
        pltpu.make_async_copy(vr.at[c], vr.at[c], a_recv.at[c]).wait()
        fields = vr[c].reshape(MODES * 8, COLS)
        phys[c] = mm3(fields, fh[...], fl[...]).reshape(MODES, 8, POINTS)
        def stress_band(band, sums):
            sums = list(sums)
            for row in range(BAND):
                mine = phys[c, band * BAND + row] * (inv_s[band * BAND + row] == LOW).astype(F32)
                for j in range(LOW):
                    sums[j] = sums[j] + mine * phys[1, nb_s[band, row, j]]
            return tuple(sums)

        zeros = tuple(jnp.zeros((8, POINTS), F32) for _ in range(LOW))
        stress = jnp.concatenate(lax.fori_loop(0, NKX, stress_band, zeros), axis=0)
        strs[re, c] = mm3(stress * (1.0 / NREAL), bh[...], bl[...])
        for d in range(1, NREAL):
            pltpu.make_async_remote_copy(
                strs.at[re, c],
                strs.at[re, c],
                st_send.at[c],
                st_recv.at[c],
                device_id=(kx, ht, lax.rem(re + d, NREAL)),
                device_id_type=MESH,
            ).start()
        low_1 = [phys[1, low_s[j]] for j in range(LOW)]
        low_c = low_1 if c == 1 else [phys[c, low_s[j]] for j in range(LOW)]

        def high_band(band, _):
            for row in range(BAND):
                high = (inv_s[band * BAND + row] == LOW).astype(F32)
                first, second = [], []
                for j in range(LOW):
                    near = nb_s[band, row, j]
                    first.append(low_c[j] * phys[1, near])
                    if c != 1:
                        second.append(low_1[j] * phys[c, near])
                total = functools.reduce(lambda a, b: a + b, first)
                total = total + (total if c == 1 else functools.reduce(lambda a, b: a + b, second))
                hl[band * BAND + row] = total * high
            return 0

        lax.fori_loop(0, NKX, high_band, 0)
        nl[c] = mm3(hl[...].reshape(MODES * 8, POINTS), bh[...], bl[...]).reshape(MODES, 8, COLS)

    def forced(c):
        pltpu.make_async_copy(strs.at[pl.ds(0, 3), 0], strs.at[pl.ds(0, 3), 0], st_recv.at[c]).wait()
        summed = (strs[0, c] + strs[1, c]) + (strs[2, c] + strs[3, c])
        zlow[c, pl.ds(0, LOW)] = summed.reshape(LOW, 8, COLS)
        half_lane = lax.broadcasted_iota(jnp.int32, (8, COLS), 1) // 2

        def one_band(band, _):
            for row in range(BAND):
                m = band * BAND + row
                gain = jnp.where(half_lane < cnt_s[band, row], F32(dt_step), F32(0.0))
                upd[pl.ds(m * 8, 8), :] = vr[c, m] + gain * (nl[c, m] + zlow[c, inv_s[m]])
            return 0

        lax.fori_loop(0, NKX, one_band, 0)
        rows = [
            upd[pl.ds(a * 4 + 2 * tile + y, MODES, stride=8), :]
            for tile in range(2)
            for a in range(2)
            for y in range(2)
        ]
        hi, lo = split(jnp.concatenate(rows, axis=0))
        turned = mm_nt(oh[...], hi) + mm_nt(oh[...], lo)
        odd = (lax.broadcasted_iota(jnp.int32, (SLOTS, 128), 1) // 32) % 2 == 1
        for tile in range(2):
            even_p = turned[:SLOTS, tile * 128 : tile * 128 + 128]
            odd_p = turned[SLOTS:, tile * 128 : tile * 128 + 128]
            first = jnp.where(odd, pltpu.roll(odd_p, 32, 1), even_p)
            second = jnp.where(odd, odd_p, pltpu.roll(even_p, 96, 1))
            snd[c, pl.ds(2 * tile, SLOTS, stride=4), :] = first
            snd[c, pl.ds(2 * tile + 1, SLOTS, stride=4), :] = second
        pltpu.make_async_copy(
            snd.at[c, pl.ds(slot * 4, 4), :], ubuf.at[c, pl.ds(source * 4, 4), :], b_recv.at[c]
        ).start()

        for t in range(1, SLOTS):
            to_kx, to_ht = kxs[t % NKX], hts[t // NKX]
            pltpu.make_async_remote_copy(
                snd.at[c, pl.ds((to_kx * NHT + to_ht) * 4, 4), :],
                ubuf.at[c, pl.ds(source * 4, 4), :],
                b_send.at[c],
                b_recv.at[c],
                device_id=(to_kx, to_ht, re),
                device_id_type=MESH,
            ).start()

    first_half = lax.broadcasted_iota(jnp.int32, (MODES, 128), 1) < 64

    def solved(c):
        pltpu.make_async_copy(ubuf.at[c], ubuf.at[c], b_recv.at[c]).wait()
        given = ubuf[c]
        swapped = pltpu.roll(given, 64, 1)
        pieces = []
        for block in range(NHT):
            pieces += [given[block * 32 : block * 32 + 32], swapped[block * 32 : block * 32 + 32]]
        fields = jnp.concatenate(pieces, axis=0).T[:64]
        answer = mm3(fields, hth[...], htl[...])
        for tile in range(4):
            even_p = answer[:MODES, tile * 128 : tile * 128 + 128]
            odd_p = answer[MODES:, tile * 128 : tile * 128 + 128]
            wsnd[c, pl.ds((2 * tile) * MODES, MODES), :] = jnp.where(
                first_half, even_p, pltpu.roll(odd_p, 64, 1)
            )
            wsnd[c, pl.ds((2 * tile + 1) * MODES, MODES), :] = jnp.where(
                first_half, pltpu.roll(even_p, 64, 1), odd_p
            )
        pltpu.make_async_copy(
            wsnd.at[c, pl.ds(ht * MODES + kx * 4, 4), :], rbuf.at[c, pl.ds(slot * 4, 4), :], c_recv.at[c]
        ).start()

        for t in range(1, SLOTS):
            to_kx, to_ht = kxs[t % NKX], hts[t // NKX]
            pltpu.make_async_remote_copy(
                wsnd.at[c, pl.ds(to_ht * MODES + to_kx * 4, 4), :],
                rbuf.at[c, pl.ds(slot * 4, 4), :],
                c_send.at[c],
                c_recv.at[c],
                device_id=(to_kx, to_ht, re),
                device_id_type=MESH,
            ).start()

    def placed(c):
        pltpu.make_async_copy(rbuf.at[c], rbuf.at[c], c_recv.at[c]).wait()
        low_half = lax.broadcasted_iota(jnp.int32, (SLOTS, 128), 1) < 64
        columns = []
        for pair in range(2):
            one = rbuf[c, pl.ds(2 * pair, SLOTS, stride=4), :]
            two = rbuf[c, pl.ds(2 * pair + 1, SLOTS, stride=4), :]
            columns.append(
                jnp.concatenate(
                    [
                        jnp.where(low_half, one, pltpu.roll(two, 64, 1)),
                        jnp.where(low_half, pltpu.roll(one, 64, 1), two),
                    ],
                    axis=0,
                )
            )
        hi, lo = split(jnp.concatenate(columns, axis=1))
        back = mm(oht[...], hi) + mm(oht[...], lo)
        for pair in range(2):
            out[c, 0, pl.ds(2 * pair, 2), :, :] = back[:, pair * 128 : pair * 128 + 128].T.reshape(2, ROWS, COLS)

    products(1)
    products(0)
    forced(1)
    products(2)
    forced(0)
    forced(2)
    for c in ORDER:
        solved(c)
    for c in ORDER:
        placed(c)

    pltpu.make_async_copy(nb_s.at[pl.ds(0, 7)], nb_s.at[pl.ds(0, 7)], i_send.at[0]).wait()
    pltpu.make_async_copy(cnt_s.at[pl.ds(0, 7)], cnt_s.at[pl.ds(0, 7)], i_send.at[1]).wait()
    for c in range(COMP):
        sent = vr.at[c, pl.ds(0, MODES - BAND)]
        pltpu.make_async_copy(sent, sent, a_send.at[c]).wait()
        sent = strs.at[pl.ds(0, NREAL - 1), c]
        pltpu.make_async_copy(sent, sent, st_send.at[c]).wait()
        sent = snd.at[c, pl.ds(0, 252), :]
        pltpu.make_async_copy(sent, sent, b_send.at[c]).wait()
        sent = wsnd.at[c, pl.ds(0, 252), :]
        pltpu.make_async_copy(sent, sent, c_send.at[c]).wait()


def local(velocity, low_index, neighbours, owner_map, mode_counts, helmholtz):
    tables = [jnp.asarray(t) for t in spanwise_tables()]
    hbm = pl.BlockSpec(memory_space=pl.ANY)
    smem = pl.BlockSpec(memory_space=pltpu.SMEM)
    vmem = pl.BlockSpec(memory_space=pltpu.VMEM)
    dma = pltpu.SemaphoreType.DMA
    held = pl.pallas_call(
        kernel,
        out_shape=pltpu.VMEM(velocity.shape, F32),
        in_specs=[hbm, smem, hbm, smem, hbm, hbm, hbm, hbm, hbm, hbm],
        out_specs=vmem,
        scratch_shapes=[
            pltpu.VMEM((COMP, MODES, 8, COLS), F32),
            pltpu.VMEM((COMP, MODES, 8, POINTS), F32),
            pltpu.VMEM((MODES, 8, POINTS), F32),
            pltpu.VMEM((COMP, MODES, 8, COLS), F32),
            pltpu.VMEM((MODES * 8, COLS), F32),
            pltpu.VMEM((COMP, 256, 128), F32),
            pltpu.VMEM((COMP, 256, 128), F32),
            pltpu.VMEM((COMP, 256, 128), F32),
            pltpu.VMEM((COMP, 256, 128), F32),
            pltpu.VMEM((NREAL, COMP, LOW * 8, COLS), F32),
            pltpu.VMEM((COMP, LOW + 1, 8, COLS), F32),
            pltpu.VMEM((128, COLS), F32),
            pltpu.VMEM((128, COLS), BF16),
            pltpu.VMEM((COLS, 128), BF16),
            pltpu.VMEM((HEIGHTS, HEIGHTS), F32),
            pltpu.VMEM((HEIGHTS, HEIGHTS), BF16),
            pltpu.VMEM((HEIGHTS, HEIGHTS), BF16),
            pltpu.VMEM((COLS, POINTS), BF16),
            pltpu.VMEM((COLS, POINTS), BF16),
            pltpu.VMEM((POINTS, COLS), BF16),
            pltpu.VMEM((POINTS, COLS), BF16),
            pltpu.SMEM((NKX, BAND, LOW), jnp.int32),
            pltpu.SMEM((NKX, BAND), jnp.int32),
            pltpu.SMEM((MODES,), jnp.int32),
            dma((COMP,)),
            dma((COMP,)),
            dma((2,)),
            dma((2,)),
            dma((COMP,)),
            dma((COMP,)),
            dma((COMP,)),
            dma((COMP,)),
            dma((COMP,)),
            dma((COMP,)),
            dma((5,)),
        ],
        compiler_params=pltpu.CompilerParams(collective_id=0, has_side_effects=True),
    )(velocity, low_index, neighbours, owner_map, mode_counts, helmholtz, *tables)
    return held


def solution(mesh):
    in_specs = (
        P(None, "real", "kx", "ht", None),
        P(),
        P("kx", None),
        P(),
        P("kx"),
        P(("kx", "ht"), None, None),
    )
    out_specs = P(None, "real", "kx", "ht", None)
    return jax.shard_map(local, mesh=mesh, in_specs=in_specs, out_specs=out_specs, check_vma=False)
```

```python
import functools

import jax
import jax.numpy as jnp
import numpy as np
from jax import lax
from jax.experimental import pallas as pl
from jax.experimental.pallas import tpu as pltpu
from jax.sharding import PartitionSpec as P

MESH = pl.DeviceIdType.MESH
F32 = jnp.float32
BF16 = jnp.bfloat16

dt_step = 0.1


def ring(step, count):
    return min(step, count - step)


COMP, BAND, ROWS, COLS = 3, 4, 64, 128
NKX, NHT, NREAL = 8, 8, 4
MODES, LOW, POINTS, HEIGHTS, SLOTS = 32, 8, 256, 512, 64
ORDER = (1, 0, 2)
FAR_FIRST = (4, 3, 5, 2, 6, 1, 7)
PAIRS = [(dk, dh) for dk in range(NKX) for dh in range(NHT) if dk + dh]
PAIRS.sort(key=lambda p: (-ring(p[1] // 2, NHT // 2), -ring(p[0], NKX)))


def forward_table():
    ids = np.arange(COLS)
    wave = (ids // 2).astype(np.float32)
    spots = np.float32(2.0 * np.pi) * np.arange(POINTS).astype(np.float32) / np.float32(POINTS)
    phases = (wave[:, None] * spots[None, :]).astype(np.float64)
    forward = (np.where(ids[:, None] % 2 == 0, np.cos(phases), -np.sin(phases)) / 8.0).astype(np.float32)
    head = forward.astype(BF16)
    return np.stack([head, (forward - head.astype(np.float32)).astype(BF16)])


def split(x):
    head = x.astype(BF16)
    return head, (x - head.astype(F32)).astype(BF16)


def mm(a, b):
    return lax.dot_general(a, b, (((1,), (0,)), ((), ())), preferred_element_type=F32)


def mm_nt(a, b):
    return lax.dot_general(a, b, (((1,), (1,)), ((), ())), preferred_element_type=F32)


def mm3(x, head, tail):
    hi, lo = split(x)
    return mm(hi, head) + (mm(hi, tail) + mm(lo, head))


def kernel(
    v, low_h, nb_own, omap_h, cnt_own, helm, table,
    out,
    vr, phys, hl, nl, upd, snd, ubuf, wsnd, rbuf, strs, zlow, onehot, oh, oht, hf, hth, htl,
    ft, bh, bl, nb_s, cnt_s, inv_s, low_s, omap_s,
    a_send, a_recv, i_send, i_recv, st_send, st_recv, b_send, b_recv, c_send, c_recv, l_sem,
):
    kx, ht, re = lax.axis_index("kx"), lax.axis_index("ht"), lax.axis_index("real")
    kxs = [lax.rem(kx + d, NKX) for d in range(NKX)]
    hts = [lax.rem(ht + d, NHT) for d in range(NHT)]

    barrier = pltpu.get_barrier_semaphore()
    for d in FAR_FIRST:
        pl.semaphore_signal(barrier, 1, device_id=(kxs[d], ht, re), device_id_type=MESH)
    for d in FAR_FIRST:
        pl.semaphore_signal(barrier, 1, device_id=(kx, hts[d], re), device_id_type=MESH)
    for d in (2, 1, 3):
        pl.semaphore_signal(barrier, 1, device_id=(kx, ht, lax.rem(re + d, NREAL)), device_id_type=MESH)
    slot = kx * NHT + ht
    source = ht * NKX + kx
    pl.semaphore_wait(barrier, (NKX - 1) + (NHT - 1) + (NREAL - 1))

    def gather(c):
        for d in FAR_FIRST:
            for a in range(2):
                pltpu.make_async_remote_copy(
                    v.at[c, 0, :, pl.ds(a * 32 + kxs[d] * 4, 4), :],
                    vr.at[c, pl.ds(kx * BAND, BAND), pl.ds(a * 4, 4), :],
                    a_send,
                    a_recv.at[c],
                    device_id=(kxs[d], ht, re),
                    device_id_type=MESH,
                ).start()

    gather(ORDER[0])
    for d in FAR_FIRST:
        for own, held, i in ((nb_own, nb_s, 0), (cnt_own, cnt_s, 1)):
            pltpu.make_async_remote_copy(
                own, held.at[kx], i_send.at[i], i_recv.at[i], device_id=(kxs[d], ht, re), device_id_type=MESH
            ).start()
    for c in ORDER[1:]:
        gather(c)
    local = [
        pltpu.make_async_copy(src, dst, l_sem.at[i])
        for i, (src, dst) in enumerate(((low_h, low_s), (omap_h, omap_s), (table, ft), (helm.at[0], hf)))
    ]
    for copy in local:
        copy.start()
    for c in ORDER:
        for a in range(2):
            pltpu.make_async_copy(
                v.at[c, 0, :, pl.ds(a * 32 + kx * 4, 4), :],
                vr.at[c, pl.ds(kx * BAND, BAND), pl.ds(a * 4, 4), :],
                a_recv.at[c],
            ).start()
    pltpu.make_async_copy(nb_own, nb_s.at[kx], i_recv.at[0]).start()
    pltpu.make_async_copy(cnt_own, cnt_s.at[kx], i_recv.at[1]).start()
    for copy in local:
        copy.wait()

    lane = lax.broadcasted_iota(jnp.int32, (1, COLS), 1)

    def one_row(s, _):
        for p in range(2):
            onehot[pl.ds(p * SLOTS + s, 1), :] = (lane == 2 * omap_s[s] + p).astype(F32)
        return 0

    lax.fori_loop(0, SLOTS, one_row, 0)
    square = onehot[...]
    oh[...] = square.astype(BF16)
    oht[...] = square.T.astype(BF16)

    def one_mode(m, _):
        place = jnp.int32(LOW)
        for j in range(LOW):
            place = jnp.where(low_s[j] == m, jnp.int32(j), place)
        inv_s[m] = place
        return 0

    lax.fori_loop(0, MODES, one_mode, 0)
    for c in range(COMP):
        zlow[c, LOW] = jnp.zeros((8, COLS), F32)
    bh[...] = (ft[0].astype(F32).T * 0.5).astype(BF16)
    bl[...] = (ft[1].astype(F32).T * 0.5).astype(BF16)
    for i in range(4):
        for j in range(4):
            block = hf[pl.ds(i * 128, 128), pl.ds(j * 128, 128)].T
            head, tail = split(block)
            hth[pl.ds(j * 128, 128), pl.ds(i * 128, 128)] = head
            htl[pl.ds(j * 128, 128), pl.ds(i * 128, 128)] = tail
    pltpu.make_async_copy(nb_s, nb_s, i_recv.at[0]).wait()
    pltpu.make_async_copy(cnt_s, cnt_s, i_recv.at[1]).wait()

    def products(c):
        pltpu.make_async_copy(vr.at[c], vr.at[c], a_recv.at[c]).wait()
        fields = vr[c].reshape(MODES * 8, COLS)
        phys[c] = mm3(fields, ft[0], ft[1]).reshape(MODES, 8, POINTS)
        for part in range(2):
            members = range(part * 4, part * 4 + 4)

            def stress_band(band, sums, members=members):
                sums = list(sums)
                for row in range(BAND):
                    mine = phys[c, band * BAND + row] * (inv_s[band * BAND + row] == LOW).astype(F32)
                    for i, j in enumerate(members):
                        sums[i] = sums[i] + mine * phys[1, nb_s[band, row, j]]
                return tuple(sums)

            zeros = tuple(jnp.zeros((8, POINTS), F32) for _ in members)
            stress = jnp.concatenate(lax.fori_loop(0, NKX, stress_band, zeros), axis=0)
            here = strs.at[re, c, pl.ds(part * 32, 32)]
            here[...] = mm3(stress * (1.0 / NREAL), bh[...], bl[...])
            for d in (2, 1, 3):
                pltpu.make_async_remote_copy(
                    here,
                    here,
                    st_send,
                    st_recv.at[c],
                    device_id=(kx, ht, lax.rem(re + d, NREAL)),
                    device_id_type=MESH,
                ).start()
        low_1 = [phys[1, low_s[j]] for j in range(LOW)]
        low_c = low_1 if c == 1 else [phys[c, low_s[j]] for j in range(LOW)]

        def high_band(band, _):
            for row in range(BAND):
                high = (inv_s[band * BAND + row] == LOW).astype(F32)
                first, second = [], []
                for j in range(LOW):
                    near = nb_s[band, row, j]
                    first.append(low_c[j] * phys[1, near])
                    if c != 1:
                        second.append(low_1[j] * phys[c, near])
                total = functools.reduce(lambda a, b: a + b, first)
                total = total + (total if c == 1 else functools.reduce(lambda a, b: a + b, second))
                hl[band * BAND + row] = total * high
            return 0

        lax.fori_loop(0, NKX, high_band, 0)
        nl[c] = mm3(hl[...].reshape(MODES * 8, POINTS), bh[...], bl[...]).reshape(MODES, 8, COLS)

    def forced(c):
        pltpu.make_async_copy(strs.at[pl.ds(0, 3), 0], strs.at[pl.ds(0, 3), 0], st_recv.at[c]).wait()
        summed = (strs[0, c] + strs[1, c]) + (strs[2, c] + strs[3, c])
        zlow[c, pl.ds(0, LOW)] = summed.reshape(LOW, 8, COLS)
        half_lane = lax.broadcasted_iota(jnp.int32, (8, COLS), 1) // 2

        def one_band(band, _):
            for row in range(BAND):
                m = band * BAND + row
                gain = jnp.where(half_lane < cnt_s[band, row], F32(dt_step), F32(0.0))
                upd[pl.ds(m * 8, 8), :] = vr[c, m] + gain * (nl[c, m] + zlow[c, inv_s[m]])
            return 0

        lax.fori_loop(0, NKX, one_band, 0)
        rows = [
            upd[pl.ds(a * 4 + 2 * tile + y, MODES, stride=8), :]
            for tile in range(2)
            for a in range(2)
            for y in range(2)
        ]
        hi, lo = split(jnp.concatenate(rows, axis=0))
        turned = mm_nt(oh[...], hi) + mm_nt(oh[...], lo)
        odd = (lax.broadcasted_iota(jnp.int32, (SLOTS, 128), 1) // 32) % 2 == 1
        for tile in range(2):
            even_p = turned[:SLOTS, tile * 128 : tile * 128 + 128]
            odd_p = turned[SLOTS:, tile * 128 : tile * 128 + 128]
            first = jnp.where(odd, pltpu.roll(odd_p, 32, 1), even_p)
            second = jnp.where(odd, odd_p, pltpu.roll(even_p, 96, 1))
            snd[c, pl.ds(2 * tile, SLOTS, stride=4), :] = first
            snd[c, pl.ds(2 * tile + 1, SLOTS, stride=4), :] = second
        pltpu.make_async_copy(
            snd.at[c, pl.ds(slot * 4, 4), :], ubuf.at[c, pl.ds(source * 4, 4), :], b_recv.at[c]
        ).start()

        for dk, dh in PAIRS:
            to_kx, to_ht = kxs[dk], hts[dh]
            pltpu.make_async_remote_copy(
                snd.at[c, pl.ds((to_kx * NHT + to_ht) * 4, 4), :],
                ubuf.at[c, pl.ds(source * 4, 4), :],
                b_send,
                b_recv.at[c],
                device_id=(to_kx, to_ht, re),
                device_id_type=MESH,
            ).start()

    first_half = lax.broadcasted_iota(jnp.int32, (MODES, 128), 1) < 64

    def solved(c):
        pltpu.make_async_copy(ubuf.at[c], ubuf.at[c], b_recv.at[c]).wait()
        given = ubuf[c]
        swapped = pltpu.roll(given, 64, 1)
        pieces = []
        for block in range(NHT):
            pieces += [given[block * 32 : block * 32 + 32], swapped[block * 32 : block * 32 + 32]]
        fields = jnp.concatenate(pieces, axis=0).T[:64]
        answer = mm3(fields, hth[...], htl[...])
        for tile in range(4):
            even_p = answer[:MODES, tile * 128 : tile * 128 + 128]
            odd_p = answer[MODES:, tile * 128 : tile * 128 + 128]
            wsnd[c, pl.ds((2 * tile) * MODES, MODES), :] = jnp.where(
                first_half, even_p, pltpu.roll(odd_p, 64, 1)
            )
            wsnd[c, pl.ds((2 * tile + 1) * MODES, MODES), :] = jnp.where(
                first_half, pltpu.roll(even_p, 64, 1), odd_p
            )
        pltpu.make_async_copy(
            wsnd.at[c, pl.ds(ht * MODES + kx * 4, 4), :], rbuf.at[c, pl.ds(slot * 4, 4), :], c_recv.at[c]
        ).start()

        for dk, dh in PAIRS:
            to_kx, to_ht = kxs[dk], hts[dh]
            pltpu.make_async_remote_copy(
                wsnd.at[c, pl.ds(to_ht * MODES + to_kx * 4, 4), :],
                rbuf.at[c, pl.ds(slot * 4, 4), :],
                c_send,
                c_recv.at[c],
                device_id=(to_kx, to_ht, re),
                device_id_type=MESH,
            ).start()

    def placed(c):
        pltpu.make_async_copy(rbuf.at[c], rbuf.at[c], c_recv.at[c]).wait()
        low_half = lax.broadcasted_iota(jnp.int32, (SLOTS, 128), 1) < 64
        columns = []
        for pair in range(2):
            one = rbuf[c, pl.ds(2 * pair, SLOTS, stride=4), :]
            two = rbuf[c, pl.ds(2 * pair + 1, SLOTS, stride=4), :]
            columns.append(
                jnp.concatenate(
                    [
                        jnp.where(low_half, one, pltpu.roll(two, 64, 1)),
                        jnp.where(low_half, pltpu.roll(one, 64, 1), two),
                    ],
                    axis=0,
                )
            )
        hi, lo = split(jnp.concatenate(columns, axis=1))
        back = mm(oht[...], hi) + mm(oht[...], lo)
        for pair in range(2):
            out[c, 0, pl.ds(2 * pair, 2), :, :] = back[:, pair * 128 : pair * 128 + 128].T.reshape(2, ROWS, COLS)

    products(1)
    products(0)
    forced(1)
    products(2)
    forced(0)
    forced(2)
    for c in ORDER:
        solved(c)
    for c in ORDER:
        placed(c)

    pltpu.make_async_copy(nb_s.at[pl.ds(0, 7)], nb_s.at[pl.ds(0, 7)], i_send.at[0]).wait()
    pltpu.make_async_copy(cnt_s.at[pl.ds(0, 7)], cnt_s.at[pl.ds(0, 7)], i_send.at[1]).wait()
    for sent, sem in (
        (vr.at[:, pl.ds(0, MODES - BAND)], a_send),
        (strs.at[pl.ds(0, NREAL - 1)], st_send),
        (snd.at[:, pl.ds(0, 252), :], b_send),
        (wsnd.at[:, pl.ds(0, 252), :], c_send),
    ):
        pltpu.make_async_copy(sent, sent, sem).wait()


def local(velocity, low_index, neighbours, owner_map, mode_counts, helmholtz):
    table = jnp.asarray(forward_table())
    hbm = pl.BlockSpec(memory_space=pl.ANY)
    vmem = pl.BlockSpec(memory_space=pltpu.VMEM)
    dma = pltpu.SemaphoreType.DMA
    held = pl.pallas_call(
        kernel,
        out_shape=pltpu.VMEM(velocity.shape, F32),
        in_specs=[hbm] * 7,
        out_specs=vmem,
        scratch_shapes=[
            pltpu.VMEM((COMP, MODES, 8, COLS), F32),
            pltpu.VMEM((COMP, MODES, 8, POINTS), F32),
            pltpu.VMEM((MODES, 8, POINTS), F32),
            pltpu.VMEM((COMP, MODES, 8, COLS), F32),
            pltpu.VMEM((MODES * 8, COLS), F32),
            pltpu.VMEM((COMP, 256, 128), F32),
            pltpu.VMEM((COMP, 256, 128), F32),
            pltpu.VMEM((COMP, 256, 128), F32),
            pltpu.VMEM((COMP, 256, 128), F32),
            pltpu.VMEM((NREAL, COMP, LOW * 8, COLS), F32),
            pltpu.VMEM((COMP, LOW + 1, 8, COLS), F32),
            pltpu.VMEM((128, COLS), F32),
            pltpu.VMEM((128, COLS), BF16),
            pltpu.VMEM((COLS, 128), BF16),
            pltpu.VMEM((HEIGHTS, HEIGHTS), F32),
            pltpu.VMEM((HEIGHTS, HEIGHTS), BF16),
            pltpu.VMEM((HEIGHTS, HEIGHTS), BF16),
            pltpu.VMEM((2, COLS, POINTS), BF16),
            pltpu.VMEM((POINTS, COLS), BF16),
            pltpu.VMEM((POINTS, COLS), BF16),
            pltpu.SMEM((NKX, BAND, LOW), jnp.int32),
            pltpu.SMEM((NKX, BAND), jnp.int32),
            pltpu.SMEM((MODES,), jnp.int32),
            pltpu.SMEM((LOW,), jnp.int32),
            pltpu.SMEM((SLOTS,), jnp.int32),
            dma,
            dma((COMP,)),
            dma((2,)),
            dma((2,)),
            dma,
            dma((COMP,)),
            dma,
            dma((COMP,)),
            dma,
            dma((COMP,)),
            dma((4,)),
        ],
        compiler_params=pltpu.CompilerParams(collective_id=0, has_side_effects=True),
    )(velocity, low_index, neighbours, owner_map, mode_counts, helmholtz, table)
    return held


def solution(mesh):
    in_specs = (
        P(None, "real", "kx", "ht", None),
        P(),
        P("kx", None),
        P(),
        P("kx"),
        P(("kx", "ht"), None, None),
    )
    out_specs = P(None, "real", "kx", "ht", None)
    return jax.shard_map(local, mesh=mesh, in_specs=in_specs, out_specs=out_specs, check_vma=False)
```

```python
import functools

import jax
import jax.numpy as jnp
import numpy as np
from jax import lax
from jax.experimental import pallas as pl
from jax.experimental.pallas import tpu as pltpu
from jax.sharding import PartitionSpec as P

MESH = pl.DeviceIdType.MESH
F32 = jnp.float32
BF16 = jnp.bfloat16

dt_step = 0.1


def ring(step, count):
    return min(step, count - step)


COMP, BAND, ROWS, COLS = 3, 4, 64, 128
NKX, NHT, NREAL = 8, 8, 4
MODES, LOW, POINTS, HEIGHTS, SLOTS = 32, 8, 256, 512, 64
HIGH = MODES - LOW
ORDER = (1, 0, 2)
FAR_FIRST = (4, 3, 5, 2, 6, 1, 7)
PAIRS = [(dk, dh) for dk in range(NKX) for dh in range(NHT) if dk + dh]
PAIRS.sort(key=lambda p: (-ring(p[1] // 2, NHT // 2), -ring(p[0], NKX)))


def forward_table():
    ids = np.arange(COLS)
    wave = (ids // 2).astype(np.float32)
    spots = np.float32(2.0 * np.pi) * np.arange(POINTS).astype(np.float32) / np.float32(POINTS)
    phases = (wave[:, None] * spots[None, :]).astype(np.float64)
    forward = (np.where(ids[:, None] % 2 == 0, np.cos(phases), -np.sin(phases)) / 8.0).astype(np.float32)
    head = forward.astype(BF16)
    return np.stack([head, head, (forward - head.astype(np.float32)).astype(BF16)])


def split(x):
    head = x.astype(BF16)
    return head, (x - head.astype(F32)).astype(BF16)


def mm(a, b):
    return lax.dot_general(a, b, (((1,), (0,)), ((), ())), preferred_element_type=F32)


def mm_nt(a, b):
    return lax.dot_general(a, b, (((1,), (1,)), ((), ())), preferred_element_type=F32)


def apply_forward(x, table):
    hi, lo = split(x)
    heads = table[pl.ds(0, 2)].reshape(2 * COLS, POINTS)
    return mm(jnp.concatenate([hi, lo], axis=1), heads) + mm(hi, table[2])


def apply_backward(x, both):
    hi, lo = split(x)
    part = mm(hi, both[...])
    return part[:, :COLS] + (part[:, COLS:] + mm(lo, both[:, :COLS]))


def kernel(
    v, low_h, nb_own, omap_h, cnt_own, helm, table,
    out,
    vr, cur, phys, hl, nl, upd, snd, ubuf, lsnd, lbuf, wsnd, rbuf, strs, onehot, oh, oht, order, om, hf, ht32, hth, htl,
    ft, back_t, nb_s, cnt_b, cnt_s, perm_s, low_s, omap_s,
    a_send, a_recv, i_send, i_recv, st_send, st_recv, h_send, h_recv, b_send, b_recv, c_send, c_recv, l_sem,
):
    kx, ht, re = lax.axis_index("kx"), lax.axis_index("ht"), lax.axis_index("real")
    kxs = [lax.rem(kx + d, NKX) for d in range(NKX)]
    hts = [lax.rem(ht + d, NHT) for d in range(NHT)]

    barrier = pltpu.get_barrier_semaphore()
    for d in FAR_FIRST:
        pl.semaphore_signal(barrier, 1, device_id=(kxs[d], ht, re), device_id_type=MESH)
    for d in FAR_FIRST:
        pl.semaphore_signal(barrier, 1, device_id=(kx, hts[d], re), device_id_type=MESH)
    for d in (2, 1, 3):
        pl.semaphore_signal(barrier, 1, device_id=(kx, ht, lax.rem(re + d, NREAL)), device_id_type=MESH)
    slot = kx * NHT + ht
    source = ht * NKX + kx
    pl.semaphore_wait(barrier, (NKX - 1) + (NHT - 1) + (NREAL - 1))

    def gather(c):
        for d in FAR_FIRST:
            pltpu.make_async_remote_copy(
                v.at[c, 0, :, pl.ds(kxs[d] * 8, 8), :],
                vr.at[c, pl.ds(kx * BAND, BAND)],
                a_send,
                a_recv.at[c],
                device_id=(kxs[d], ht, re),
                device_id_type=MESH,
            ).start()

    gather(ORDER[0])
    for d in FAR_FIRST:
        for own, held, i in ((nb_own, nb_s.at[pl.ds(kx * BAND, BAND)], 0), (cnt_own, cnt_b.at[kx], 1)):
            pltpu.make_async_remote_copy(
                own, held, i_send.at[i], i_recv.at[i], device_id=(kxs[d], ht, re), device_id_type=MESH
            ).start()
    for c in ORDER[1:]:
        gather(c)
    local = [
        pltpu.make_async_copy(src, dst, l_sem.at[i])
        for i, (src, dst) in enumerate(((low_h, low_s), (omap_h, omap_s), (table, ft), (helm.at[0], hf)))
    ]
    for copy in local:
        copy.start()
    for c in ORDER:
        pltpu.make_async_copy(
            v.at[c, 0, :, pl.ds(kx * 8, 8), :], vr.at[c, pl.ds(kx * BAND, BAND)], a_recv.at[c]
        ).start()
    pltpu.make_async_copy(nb_own, nb_s.at[pl.ds(kx * BAND, BAND)], i_recv.at[0]).start()
    pltpu.make_async_copy(cnt_own, cnt_b.at[kx], i_recv.at[1]).start()
    for copy in local:
        copy.wait()

    lane = lax.broadcasted_iota(jnp.int32, (1, COLS), 1)

    def one_row(s, _):
        for p in range(2):
            onehot[pl.ds(p * SLOTS + s, 1), :] = (lane == 2 * omap_s[s] + p).astype(F32)
        return 0

    lax.fori_loop(0, SLOTS, one_row, 0)
    square = onehot[...]
    turn = square.T
    for i in range(2):
        oh[:, pl.ds(i * 128, 128)] = square.astype(BF16)
        oht[:, pl.ds(i * 128, 128)] = turn.astype(BF16)

    lows = [low_s[j] for j in range(LOW)]
    ranked = list(lows)
    for i in range(LOW):
        for j in range(i % 2, LOW - 1, 2):
            one, two = ranked[j], ranked[j + 1]
            ranked[j], ranked[j + 1] = jnp.minimum(one, two), jnp.maximum(one, two)

    def one_high(q, _):
        mode = q
        for low in ranked:
            mode = mode + (low <= mode).astype(jnp.int32)
        perm_s[q] = mode
        return 0

    lax.fori_loop(0, HIGH, one_high, 0)
    for j in range(LOW):
        perm_s[HIGH + j] = lows[j]

    def one_mode(m, _):
        place = m
        for low in lows:
            place = place - (low < m).astype(jnp.int32)
        for j, low in enumerate(lows):
            place = jnp.where(low == m, jnp.int32(HIGH + j), place)
        order[pl.ds(m, 1), :] = (lane == place).astype(F32)
        order[pl.ds(MODES + m, 1), :] = (lane == MODES + place).astype(F32)
        return 0

    lax.fori_loop(0, MODES, one_mode, 0)
    om[...] = order[:, : 2 * MODES].astype(BF16)
    back_t[:, pl.ds(0, COLS)] = (ft[0].astype(F32).T * 0.5).astype(BF16)
    back_t[:, pl.ds(COLS, COLS)] = (ft[2].astype(F32).T * 0.5).astype(BF16)
    for i in range(4):
        for j in range(4):
            ht32[i, pl.ds(j * 128, 128), :] = hf[pl.ds(i * 128, 128), pl.ds(j * 128, 128)].T
    for y in range(4):
        for a in range(2):
            for i in range(4):
                rows = [ht32[i, pl.ds(h * 64 + a * 4 + y, NKX, stride=8), :] for h in range(NHT)]
                head, tail = split(jnp.concatenate(rows, axis=0))
                hth[pl.ds((y * 2 + a) * 64, 64), pl.ds(i * 128, 128)] = head
                htl[pl.ds((y * 2 + a) * 64, 64), pl.ds(i * 128, 128)] = tail
    pltpu.make_async_copy(nb_s, nb_s, i_recv.at[0]).wait()
    pltpu.make_async_copy(cnt_b, cnt_b, i_recv.at[1]).wait()
    for m in range(MODES):
        cnt_s[m] = cnt_b[m // BAND, m % BAND]

    def products(c):
        pltpu.make_async_copy(vr.at[c], vr.at[c], a_recv.at[c]).wait()
        fields = vr[c].reshape(MODES * 8, COLS)
        cur[c] = vr[c]
        phys[c] = apply_forward(fields, ft).reshape(MODES, 8, POINTS)
        for part in range(2):
            members = range(part * 4, part * 4 + 4)

            def stress_band(band, sums, members=members):
                sums = list(sums)
                for row in range(BAND):
                    mode = perm_s[band * BAND + row]
                    mine = phys[c, mode]
                    for i, j in enumerate(members):
                        sums[i] = sums[i] + mine * phys[1, nb_s[mode, j]]
                return tuple(sums)

            zeros = tuple(jnp.zeros((8, POINTS), F32) for _ in members)
            stress = jnp.concatenate(lax.fori_loop(0, HIGH // BAND, stress_band, zeros), axis=0)
            here = strs.at[re, c, pl.ds(part * 32, 32)]
            here[...] = apply_backward(stress * (1.0 / NREAL), back_t)
            for d in (2, 1, 3):
                pltpu.make_async_remote_copy(
                    here,
                    here,
                    st_send,
                    st_recv.at[c],
                    device_id=(kx, ht, lax.rem(re + d, NREAL)),
                    device_id_type=MESH,
                ).start()
        low_1 = [phys[1, low_s[j]] for j in range(LOW)]
        low_c = low_1 if c == 1 else [phys[c, low_s[j]] for j in range(LOW)]

        def high_band(band, _):
            for row in range(BAND):
                mode = perm_s[band * BAND + row]
                first, second = [], []
                for j in range(LOW):
                    near = nb_s[mode, j]
                    first.append(low_c[j] * phys[1, near])
                    if c != 1:
                        second.append(low_1[j] * phys[c, near])
                total = functools.reduce(lambda a, b: a + b, first)
                total = total + (total if c == 1 else functools.reduce(lambda a, b: a + b, second))
                hl[band * BAND + row] = total
            return 0

        lax.fori_loop(0, HIGH // BAND, high_band, 0)
        nl[c] = apply_backward(hl[...].reshape(HIGH * 8, POINTS), back_t).reshape(HIGH, 8, COLS)

    half_lane = lax.broadcasted_iota(jnp.int32, (8, COLS), 1) // 2
    odd = (lax.broadcasted_iota(jnp.int32, (SLOTS, 128), 1) // 32) % 2 == 1

    def gain(mode):
        return jnp.where(half_lane < cnt_s[mode], F32(dt_step), F32(0.0))

    def turned(tiles):
        rows = [
            upd[pl.ds(group * 64 + a * 4 + y, 8, stride=8), :]
            for pair in tiles
            for a in range(2)
            for group in pair
            for y in range(4)
        ]
        hi, lo = split(jnp.concatenate(rows, axis=0))
        both = mm_nt(oh[...], jnp.concatenate([hi, lo], axis=1))
        given = []
        for tile in range(len(tiles)):
            even_p = both[:SLOTS, tile * 128 : tile * 128 + 128]
            odd_p = both[SLOTS:, tile * 128 : tile * 128 + 128]
            given.append(jnp.where(odd, pltpu.roll(odd_p, 32, 1), even_p))
            given.append(jnp.where(odd, odd_p, pltpu.roll(even_p, 96, 1)))
        return given

    def to_owners(given, taken, stride, count, send, recv):
        pltpu.make_async_copy(
            given.at[pl.ds(slot * stride, count), :], taken.at[pl.ds(source * stride, count), :], recv
        ).start()
        for dk, dh in PAIRS:
            to_kx, to_ht = kxs[dk], hts[dh]
            pltpu.make_async_remote_copy(
                given.at[pl.ds((to_kx * NHT + to_ht) * stride, count), :],
                taken.at[pl.ds(source * stride, count), :],
                send,
                recv,
                device_id=(to_kx, to_ht, re),
                device_id_type=MESH,
            ).start()

    def forced_high(c):
        def one_band(band, _):
            for row in range(BAND):
                q = band * BAND + row
                mode = perm_s[q]
                upd[pl.ds(q * 8, 8), :] = cur[c, mode] + gain(mode) * nl[c, q]
            return 0

        lax.fori_loop(0, HIGH // BAND, one_band, 0)
        for group, value in enumerate(turned(((0, 1), (2, 2)))[:3]):
            snd[c, pl.ds(group, SLOTS, stride=4), :] = value

    def forced_low(c):
        pltpu.make_async_copy(strs.at[pl.ds(0, 3), 0], strs.at[pl.ds(0, 3), 0], st_recv.at[c]).wait()
        summed = (strs[0, c] + strs[1, c]) + (strs[2, c] + strs[3, c])
        for j in range(LOW):
            mode = low_s[j]
            upd[pl.ds((HIGH + j) * 8, 8), :] = cur[c, mode] + gain(mode) * summed[j * 8 : j * 8 + 8]
        value = turned(((3, 3),))[0]
        if c == ORDER[2]:
            lsnd[...] = value
        else:
            snd[ORDER[ORDER.index(c) + 1], pl.ds(3, SLOTS, stride=4), :] = value

    first_half = lax.broadcasted_iota(jnp.int32, (MODES, 128), 1) < 64

    def solved(c):
        place = ORDER.index(c)
        if place == 0:
            arrived = ubuf.at[c, pl.ds(0, 3 * SLOTS), :]
            pltpu.make_async_copy(arrived, arrived, h_recv.at[c]).wait()
        if place < 2:
            arrived = ubuf.at[ORDER[place + 1]]
            pltpu.make_async_copy(arrived, arrived, h_recv.at[ORDER[place + 1]]).wait()
        else:
            pltpu.make_async_copy(lbuf, lbuf, b_recv).wait()
        groups = []
        for group in range(4):
            if group < 3:
                given = ubuf[c, pl.ds(group, SLOTS, stride=4), :]
            else:
                given = lbuf[...] if place == 2 else ubuf[ORDER[place + 1], pl.ds(3, SLOTS, stride=4), :]
            groups.append(jnp.concatenate([given, pltpu.roll(given, 64, 1)], axis=0).T[:64])
        fields = jnp.concatenate(
            [
                jnp.concatenate([groups[g][(p * 4 + y) * 8 : (p * 4 + y) * 8 + 8] for y in range(4)], axis=1)
                for p in range(2)
                for g in range(4)
            ],
            axis=0,
        )
        hi, lo = split(fields)
        hi = mm(om[...], hi).astype(BF16)
        lo = mm(om[...], lo).astype(BF16)
        part = mm(jnp.concatenate([hi, lo], axis=0), hth[...])
        answer = part[: 2 * MODES] + (mm(hi, htl[...]) + part[2 * MODES :])
        for tile in range(4):
            even_p = answer[:MODES, tile * 128 : tile * 128 + 128]
            odd_p = answer[MODES:, tile * 128 : tile * 128 + 128]
            wsnd[c, pl.ds((2 * tile) * MODES, MODES), :] = jnp.where(
                first_half, even_p, pltpu.roll(odd_p, 64, 1)
            )
            wsnd[c, pl.ds((2 * tile + 1) * MODES, MODES), :] = jnp.where(
                first_half, pltpu.roll(even_p, 64, 1), odd_p
            )
        pltpu.make_async_copy(
            wsnd.at[c, pl.ds(ht * MODES + kx * 4, 4), :], rbuf.at[c, pl.ds(slot * 4, 4), :], c_recv.at[c]
        ).start()

        for dk, dh in PAIRS:
            to_kx, to_ht = kxs[dk], hts[dh]
            pltpu.make_async_remote_copy(
                wsnd.at[c, pl.ds(to_ht * MODES + to_kx * 4, 4), :],
                rbuf.at[c, pl.ds(slot * 4, 4), :],
                c_send,
                c_recv.at[c],
                device_id=(to_kx, to_ht, re),
                device_id_type=MESH,
            ).start()

    def placed(c):
        pltpu.make_async_copy(rbuf.at[c], rbuf.at[c], c_recv.at[c]).wait()
        low_half = lax.broadcasted_iota(jnp.int32, (SLOTS, 128), 1) < 64
        columns = []
        for pair in range(2):
            one = rbuf[c, pl.ds(2 * pair, SLOTS, stride=4), :]
            two = rbuf[c, pl.ds(2 * pair + 1, SLOTS, stride=4), :]
            columns.append(
                jnp.concatenate(
                    [
                        jnp.where(low_half, one, pltpu.roll(two, 64, 1)),
                        jnp.where(low_half, pltpu.roll(one, 64, 1), two),
                    ],
                    axis=0,
                )
            )
        hi, lo = split(jnp.concatenate(columns, axis=1))
        back = mm(oht[...], jnp.concatenate([hi, lo], axis=0))
        for pair in range(2):
            out[c, 0, pl.ds(2 * pair, 2), :, :] = back[:, pair * 128 : pair * 128 + 128].T.reshape(2, ROWS, COLS)

    one, two, three = ORDER
    products(one)
    forced_high(one)
    to_owners(snd.at[one], ubuf.at[one], 4, 3, h_send, h_recv.at[one])
    products(two)
    forced_high(two)
    forced_low(one)
    to_owners(snd.at[two], ubuf.at[two], 4, 4, h_send, h_recv.at[two])
    products(three)
    forced_high(three)
    forced_low(two)
    to_owners(snd.at[three], ubuf.at[three], 4, 4, h_send, h_recv.at[three])
    forced_low(three)
    to_owners(lsnd, lbuf, 1, 1, b_send, b_recv)
    for c in ORDER:
        solved(c)
    for c in ORDER:
        placed(c)

    pltpu.make_async_copy(nb_s.at[pl.ds(0, 28)], nb_s.at[pl.ds(0, 28)], i_send.at[0]).wait()
    pltpu.make_async_copy(cnt_b.at[pl.ds(0, 7)], cnt_b.at[pl.ds(0, 7)], i_send.at[1]).wait()
    for sent, sem in (
        (vr.at[:, pl.ds(0, MODES - BAND)], a_send),
        (strs.at[pl.ds(0, NREAL - 1)], st_send),
        (snd.at[:, pl.ds(0, 231), :], h_send),
        (lsnd.at[pl.ds(0, 63), :], b_send),
        (wsnd.at[:, pl.ds(0, 252), :], c_send),
    ):
        pltpu.make_async_copy(sent, sent, sem).wait()


def local(velocity, low_index, neighbours, owner_map, mode_counts, helmholtz):
    table = jnp.asarray(forward_table())
    hbm = pl.BlockSpec(memory_space=pl.ANY)
    vmem = pl.BlockSpec(memory_space=pltpu.VMEM)
    dma = pltpu.SemaphoreType.DMA
    held = pl.pallas_call(
        kernel,
        out_shape=pltpu.VMEM(velocity.shape, F32),
        in_specs=[hbm] * 7,
        out_specs=vmem,
        scratch_shapes=[
            pltpu.VMEM((COMP, MODES, 8, COLS), F32),
            pltpu.VMEM((COMP, MODES, 8, COLS), F32),
            pltpu.VMEM((COMP, MODES, 8, POINTS), F32),
            pltpu.VMEM((HIGH, 8, POINTS), F32),
            pltpu.VMEM((COMP, HIGH, 8, COLS), F32),
            pltpu.VMEM((MODES * 8, COLS), F32),
            pltpu.VMEM((COMP, 256, 128), F32),
            pltpu.VMEM((COMP, 256, 128), F32),
            pltpu.VMEM((SLOTS, 128), F32),
            pltpu.VMEM((SLOTS, 128), F32),
            pltpu.VMEM((COMP, 256, 128), F32),
            pltpu.VMEM((COMP, 256, 128), F32),
            pltpu.VMEM((NREAL, COMP, LOW * 8, COLS), F32),
            pltpu.VMEM((128, COLS), F32),
            pltpu.VMEM((128, 2 * COLS), BF16),
            pltpu.VMEM((COLS, 256), BF16),
            pltpu.VMEM((2 * MODES, 128), F32),
            pltpu.VMEM((2 * MODES, 2 * MODES), BF16),
            pltpu.VMEM((HEIGHTS, HEIGHTS), F32),
            pltpu.VMEM((4, HEIGHTS, 128), F32),
            pltpu.VMEM((HEIGHTS, HEIGHTS), BF16),
            pltpu.VMEM((HEIGHTS, HEIGHTS), BF16),
            pltpu.VMEM((3, COLS, POINTS), BF16),
            pltpu.VMEM((POINTS, 2 * COLS), BF16),
            pltpu.SMEM((MODES, LOW), jnp.int32),
            pltpu.SMEM((NKX, BAND), jnp.int32),
            pltpu.SMEM((MODES,), jnp.int32),
            pltpu.SMEM((MODES,), jnp.int32),
            pltpu.SMEM((LOW,), jnp.int32),
            pltpu.SMEM((SLOTS,), jnp.int32),
            dma,
            dma((COMP,)),
            dma((2,)),
            dma((2,)),
            dma,
            dma((COMP,)),
            dma,
            dma((COMP,)),
            dma,
            dma,
            dma,
            dma((COMP,)),
            dma((4,)),
        ],
        compiler_params=pltpu.CompilerParams(collective_id=0, has_side_effects=True),
    )(velocity, low_index, neighbours, owner_map, mode_counts, helmholtz, table)
    return held


def solution(mesh):
    in_specs = (
        P(None, "real", "kx", "ht", None),
        P(),
        P("kx", None),
        P(),
        P("kx"),
        P(("kx", "ht"), None, None),
    )
    out_specs = P(None, "real", "kx", "ht", None)
    return jax.shard_map(local, mesh=mesh, in_specs=in_specs, out_specs=out_specs, check_vma=False)
```

```python
import functools

import jax
import jax.numpy as jnp
import numpy as np
from jax import lax
from jax.experimental import pallas as pl
from jax.experimental.pallas import tpu as pltpu
from jax.sharding import PartitionSpec as P

MESH = pl.DeviceIdType.MESH
F32 = jnp.float32
BF16 = jnp.bfloat16

dt_step = 0.1


def ring(step, count):
    return min(step, count - step)


COMP, BAND, ROWS, COLS = 3, 4, 64, 128
NKX, NHT, NREAL = 8, 8, 4
MODES, LOW, POINTS, HEIGHTS, SLOTS = 32, 8, 256, 512, 64
HIGH = MODES - LOW
ORDER = (1, 0, 2)
FAR_FIRST = (4, 3, 5, 2, 6, 1, 7)
PAIRS = [(dk, dh) for dk in range(NKX) for dh in range(NHT) if dk + dh]
PAIRS.sort(key=lambda p: (-ring(p[1] // 2, NHT // 2), -ring(p[0], NKX)))


def forward_table():
    ids = np.arange(COLS)
    wave = (ids // 2).astype(np.float32)
    spots = np.float32(2.0 * np.pi) * np.arange(POINTS).astype(np.float32) / np.float32(POINTS)
    phases = (wave[:, None] * spots[None, :]).astype(np.float64)
    forward = (np.where(ids[:, None] % 2 == 0, np.cos(phases), -np.sin(phases)) / 8.0).astype(np.float32)
    head = forward.astype(BF16)
    return np.stack([head, head, (forward - head.astype(np.float32)).astype(BF16)])


def split(x):
    head = x.astype(BF16)
    return head, (x - head.astype(F32)).astype(BF16)


def mm(a, b):
    return lax.dot_general(a, b, (((1,), (0,)), ((), ())), preferred_element_type=F32)


def mm_nt(a, b):
    return lax.dot_general(a, b, (((1,), (1,)), ((), ())), preferred_element_type=F32)


def apply_forward(x, table):
    hi, lo = split(x)
    heads = table[pl.ds(0, 2)].reshape(2 * COLS, POINTS)
    return mm(jnp.concatenate([hi, lo], axis=1), heads) + mm(hi, table[2])


def apply_backward(x, both):
    hi, lo = split(x)
    part = mm(hi, both[...])
    return part[:, :COLS] + (part[:, COLS:] + mm(lo, both[:, :COLS]))


def kernel(
    v, low_h, nb_own, omap_h, cnt_own, helm, table,
    out,
    vr, cur, phys, hl, nl, upd, snd, ubuf, lsnd, lbuf, fsnd, fbuf, wsnd, rbuf, strs, onehot, oh, oht, order, om, hf, ht32, hth, htl,
    ft, back_t, nb_s, cnt_b, cnt_s, perm_s, low_s, omap_s,
    a_send, a_recv, i_send, i_recv, st_send, st_recv, h_send, h_recv, b_send, b_recv, c_send, c_recv, l_sem,
):
    kx, ht, re = lax.axis_index("kx"), lax.axis_index("ht"), lax.axis_index("real")
    kxs = [lax.rem(kx + d, NKX) for d in range(NKX)]
    hts = [lax.rem(ht + d, NHT) for d in range(NHT)]

    barrier = pltpu.get_barrier_semaphore()
    for d in FAR_FIRST:
        pl.semaphore_signal(barrier, 1, device_id=(kxs[d], ht, re), device_id_type=MESH)
    for d in FAR_FIRST:
        pl.semaphore_signal(barrier, 1, device_id=(kx, hts[d], re), device_id_type=MESH)
    for d in (2, 1, 3):
        pl.semaphore_signal(barrier, 1, device_id=(kx, ht, lax.rem(re + d, NREAL)), device_id_type=MESH)
    slot = kx * NHT + ht
    source = ht * NKX + kx
    pl.semaphore_wait(barrier, (NKX - 1) + (NHT - 1) + (NREAL - 1))

    def gather(c):
        for d in FAR_FIRST:
            pltpu.make_async_remote_copy(
                v.at[c, 0, :, pl.ds(kxs[d] * 8, 8), :],
                vr.at[c, pl.ds(kx * BAND, BAND)],
                a_send,
                a_recv.at[c],
                device_id=(kxs[d], ht, re),
                device_id_type=MESH,
            ).start()

    gather(ORDER[0])
    for d in FAR_FIRST:
        for own, held, i in ((nb_own, nb_s.at[pl.ds(kx * BAND, BAND)], 0), (cnt_own, cnt_b.at[kx], 1)):
            pltpu.make_async_remote_copy(
                own, held, i_send.at[i], i_recv.at[i], device_id=(kxs[d], ht, re), device_id_type=MESH
            ).start()
    for c in ORDER[1:]:
        gather(c)
    local = [
        pltpu.make_async_copy(src, dst, l_sem.at[i])
        for i, (src, dst) in enumerate(((low_h, low_s), (omap_h, omap_s), (table, ft), (helm.at[0], hf)))
    ]
    for copy in local:
        copy.start()
    for c in ORDER:
        pltpu.make_async_copy(
            v.at[c, 0, :, pl.ds(kx * 8, 8), :], vr.at[c, pl.ds(kx * BAND, BAND)], a_recv.at[c]
        ).start()
    pltpu.make_async_copy(nb_own, nb_s.at[pl.ds(kx * BAND, BAND)], i_recv.at[0]).start()
    pltpu.make_async_copy(cnt_own, cnt_b.at[kx], i_recv.at[1]).start()
    for copy in local:
        copy.wait()

    lane = lax.broadcasted_iota(jnp.int32, (1, COLS), 1)

    def one_row(s, _):
        for p in range(2):
            onehot[pl.ds(p * SLOTS + s, 1), :] = (lane == 2 * omap_s[s] + p).astype(F32)
        return 0

    lax.fori_loop(0, SLOTS, one_row, 0)
    square = onehot[...]
    turn = square.T
    for i in range(2):
        oh[:, pl.ds(i * 128, 128)] = square.astype(BF16)
        oht[:, pl.ds(i * 128, 128)] = turn.astype(BF16)

    lows = [low_s[j] for j in range(LOW)]
    ranked = list(lows)
    for i in range(LOW):
        for j in range(i % 2, LOW - 1, 2):
            one, two = ranked[j], ranked[j + 1]
            ranked[j], ranked[j + 1] = jnp.minimum(one, two), jnp.maximum(one, two)

    def one_high(q, _):
        mode = q
        for low in ranked:
            mode = mode + (low <= mode).astype(jnp.int32)
        perm_s[q] = mode
        return 0

    lax.fori_loop(0, HIGH, one_high, 0)
    for j in range(LOW):
        perm_s[HIGH + j] = lows[j]

    def one_mode(m, _):
        place = m
        for low in lows:
            place = place - (low < m).astype(jnp.int32)
        for j, low in enumerate(lows):
            place = jnp.where(low == m, jnp.int32(HIGH + j), place)
        order[pl.ds(m, 1), :] = (lane == place).astype(F32)
        order[pl.ds(MODES + m, 1), :] = (lane == MODES + place).astype(F32)
        return 0

    lax.fori_loop(0, MODES, one_mode, 0)
    om[...] = order[:, : 2 * MODES].astype(BF16)
    back_t[:, pl.ds(0, COLS)] = (ft[0].astype(F32).T * 0.5).astype(BF16)
    back_t[:, pl.ds(COLS, COLS)] = (ft[2].astype(F32).T * 0.5).astype(BF16)
    for i in range(4):
        for j in range(4):
            ht32[i, pl.ds(j * 128, 128), :] = hf[pl.ds(i * 128, 128), pl.ds(j * 128, 128)].T
    for y in range(4):
        for a in range(2):
            for i in range(4):
                rows = [ht32[i, pl.ds(h * 64 + a * 4 + y, NKX, stride=8), :] for h in range(NHT)]
                head, tail = split(jnp.concatenate(rows, axis=0))
                hth[pl.ds((y * 2 + a) * 64, 64), pl.ds(i * 128, 128)] = head
                htl[pl.ds((y * 2 + a) * 64, 64), pl.ds(i * 128, 128)] = tail
    pltpu.make_async_copy(nb_s, nb_s, i_recv.at[0]).wait()
    pltpu.make_async_copy(cnt_b, cnt_b, i_recv.at[1]).wait()
    for m in range(MODES):
        cnt_s[m] = cnt_b[m // BAND, m % BAND]

    def products(c):
        pltpu.make_async_copy(vr.at[c], vr.at[c], a_recv.at[c]).wait()
        fields = vr[c].reshape(MODES * 8, COLS)
        cur[c] = vr[c]
        phys[c] = apply_forward(fields, ft).reshape(MODES, 8, POINTS)
        def stress_band(band, sums):
            sums = list(sums)
            for row in range(BAND):
                mode = perm_s[band * BAND + row]
                mine = phys[c, mode]
                for j in range(LOW):
                    sums[j] = sums[j] + mine * phys[1, nb_s[mode, j]]
            return tuple(sums)

        zeros = tuple(jnp.zeros((8, POINTS), F32) for _ in range(LOW))
        stress = jnp.concatenate(lax.fori_loop(0, HIGH // BAND, stress_band, zeros), axis=0)
        here = strs.at[re, c]
        here[...] = apply_backward(stress * (1.0 / NREAL), back_t)
        for d in (2, 1, 3):
            pltpu.make_async_remote_copy(
                here,
                here,
                st_send,
                st_recv.at[c],
                device_id=(kx, ht, lax.rem(re + d, NREAL)),
                device_id_type=MESH,
            ).start()
        low_1 = [phys[1, low_s[j]] for j in range(LOW)]
        low_c = low_1 if c == 1 else [phys[c, low_s[j]] for j in range(LOW)]

        def high_band(band, _):
            for row in range(BAND):
                mode = perm_s[band * BAND + row]
                first, second = [], []
                for j in range(LOW):
                    near = nb_s[mode, j]
                    first.append(low_c[j] * phys[1, near])
                    if c != 1:
                        second.append(low_1[j] * phys[c, near])
                total = functools.reduce(lambda a, b: a + b, first)
                total = total + (total if c == 1 else functools.reduce(lambda a, b: a + b, second))
                hl[band * BAND + row] = total
            return 0

        lax.fori_loop(0, HIGH // BAND, high_band, 0)
        nl[c] = apply_backward(hl[...].reshape(HIGH * 8, POINTS), back_t).reshape(HIGH, 8, COLS)

    half_lane = lax.broadcasted_iota(jnp.int32, (8, COLS), 1) // 2
    odd = (lax.broadcasted_iota(jnp.int32, (SLOTS, 128), 1) // 32) % 2 == 1

    def gain(mode):
        return jnp.where(half_lane < cnt_s[mode], F32(dt_step), F32(0.0))

    def turned(tiles):
        rows = [
            upd[pl.ds(group * 64 + a * 4 + y, 8, stride=8), :]
            for pair in tiles
            for a in range(2)
            for group in pair
            for y in range(4)
        ]
        hi, lo = split(jnp.concatenate(rows, axis=0))
        both = mm_nt(oh[...], jnp.concatenate([hi, lo], axis=1))
        given = []
        for tile in range(len(tiles)):
            even_p = both[:SLOTS, tile * 128 : tile * 128 + 128]
            odd_p = both[SLOTS:, tile * 128 : tile * 128 + 128]
            given.append(jnp.where(odd, pltpu.roll(odd_p, 32, 1), even_p))
            given.append(jnp.where(odd, odd_p, pltpu.roll(even_p, 96, 1)))
        return given

    def to_owners(given, taken, stride, count, send, recv):
        pltpu.make_async_copy(
            given.at[pl.ds(slot * stride, count), :], taken.at[pl.ds(source * stride, count), :], recv
        ).start()
        for dk, dh in PAIRS:
            to_kx, to_ht = kxs[dk], hts[dh]
            pltpu.make_async_remote_copy(
                given.at[pl.ds((to_kx * NHT + to_ht) * stride, count), :],
                taken.at[pl.ds(source * stride, count), :],
                send,
                recv,
                device_id=(to_kx, to_ht, re),
                device_id_type=MESH,
            ).start()

    def forced_high(c):
        def one_band(band, _):
            for row in range(BAND):
                q = band * BAND + row
                mode = perm_s[q]
                upd[pl.ds(q * 8, 8), :] = cur[c, mode] + gain(mode) * nl[c, q]
            return 0

        lax.fori_loop(0, HIGH // BAND, one_band, 0)
        for group, value in enumerate(turned(((0, 1), (2, 2)))[:3]):
            snd[c, pl.ds(group, SLOTS, stride=4), :] = value

    def forced_low(c):
        pltpu.make_async_copy(strs.at[pl.ds(0, 3), 0], strs.at[pl.ds(0, 3), 0], st_recv.at[c]).wait()
        summed = (strs[0, c] + strs[1, c]) + (strs[2, c] + strs[3, c])
        for j in range(LOW):
            mode = low_s[j]
            upd[pl.ds((HIGH + j) * 8, 8), :] = cur[c, mode] + gain(mode) * summed[j * 8 : j * 8 + 8]
        value = turned(((3, 3),))[0]
        if c == ORDER[2]:
            lsnd[...] = value
        elif c == ORDER[0]:
            fsnd[...] = value
        else:
            snd[ORDER[ORDER.index(c) + 1], pl.ds(3, SLOTS, stride=4), :] = value

    first_half = lax.broadcasted_iota(jnp.int32, (MODES, 128), 1) < 64

    def solved(c):
        place = ORDER.index(c)
        if place == 0:
            arrived = ubuf.at[c, pl.ds(0, 3 * SLOTS), :]
            pltpu.make_async_copy(arrived, arrived, h_recv.at[c]).wait()
            pltpu.make_async_copy(fbuf, fbuf, b_recv.at[0]).wait()
        elif place == 1:
            arrived = ubuf.at[c, pl.ds(0, 3 * SLOTS), :]
            pltpu.make_async_copy(arrived, arrived, h_recv.at[c]).wait()
            pltpu.make_async_copy(ubuf.at[ORDER[2]], ubuf.at[ORDER[2]], h_recv.at[ORDER[2]]).wait()
        else:
            pltpu.make_async_copy(lbuf, lbuf, b_recv.at[1]).wait()
        groups = []
        for group in range(4):
            if group < 3:
                given = ubuf[c, pl.ds(group, SLOTS, stride=4), :]
            else:
                low = (fbuf, None, lbuf)[place]
                given = ubuf[ORDER[2], pl.ds(3, SLOTS, stride=4), :] if place == 1 else low[...]
            groups.append(jnp.concatenate([given, pltpu.roll(given, 64, 1)], axis=0).T[:64])
        fields = jnp.concatenate(
            [
                jnp.concatenate([groups[g][(p * 4 + y) * 8 : (p * 4 + y) * 8 + 8] for y in range(4)], axis=1)
                for p in range(2)
                for g in range(4)
            ],
            axis=0,
        )
        hi, lo = split(fields)
        hi = mm(om[...], hi).astype(BF16)
        lo = mm(om[...], lo).astype(BF16)
        part = mm(jnp.concatenate([hi, lo], axis=0), hth[...])
        answer = part[: 2 * MODES] + (mm(hi, htl[...]) + part[2 * MODES :])
        for tile in range(4):
            even_p = answer[:MODES, tile * 128 : tile * 128 + 128]
            odd_p = answer[MODES:, tile * 128 : tile * 128 + 128]
            wsnd[c, pl.ds((2 * tile) * MODES, MODES), :] = jnp.where(
                first_half, even_p, pltpu.roll(odd_p, 64, 1)
            )
            wsnd[c, pl.ds((2 * tile + 1) * MODES, MODES), :] = jnp.where(
                first_half, pltpu.roll(even_p, 64, 1), odd_p
            )
        pltpu.make_async_copy(
            wsnd.at[c, pl.ds(ht * MODES + kx * 4, 4), :], rbuf.at[c, pl.ds(slot * 4, 4), :], c_recv.at[c]
        ).start()

        for dk, dh in PAIRS:
            to_kx, to_ht = kxs[dk], hts[dh]
            pltpu.make_async_remote_copy(
                wsnd.at[c, pl.ds(to_ht * MODES + to_kx * 4, 4), :],
                rbuf.at[c, pl.ds(slot * 4, 4), :],
                c_send,
                c_recv.at[c],
                device_id=(to_kx, to_ht, re),
                device_id_type=MESH,
            ).start()

    def placed(c):
        pltpu.make_async_copy(rbuf.at[c], rbuf.at[c], c_recv.at[c]).wait()
        low_half = lax.broadcasted_iota(jnp.int32, (SLOTS, 128), 1) < 64
        columns = []
        for pair in range(2):
            one = rbuf[c, pl.ds(2 * pair, SLOTS, stride=4), :]
            two = rbuf[c, pl.ds(2 * pair + 1, SLOTS, stride=4), :]
            columns.append(
                jnp.concatenate(
                    [
                        jnp.where(low_half, one, pltpu.roll(two, 64, 1)),
                        jnp.where(low_half, pltpu.roll(one, 64, 1), two),
                    ],
                    axis=0,
                )
            )
        hi, lo = split(jnp.concatenate(columns, axis=1))
        back = mm(oht[...], jnp.concatenate([hi, lo], axis=0))
        for pair in range(2):
            out[c, 0, pl.ds(2 * pair, 2), :, :] = back[:, pair * 128 : pair * 128 + 128].T.reshape(2, ROWS, COLS)

    one, two, three = ORDER
    products(one)
    forced_high(one)
    to_owners(snd.at[one], ubuf.at[one], 4, 3, h_send, h_recv.at[one])
    products(two)
    forced_high(two)
    to_owners(snd.at[two], ubuf.at[two], 4, 3, h_send, h_recv.at[two])
    forced_low(one)
    to_owners(fsnd, fbuf, 1, 1, b_send.at[0], b_recv.at[0])
    products(three)
    forced_high(three)
    forced_low(two)
    to_owners(snd.at[three], ubuf.at[three], 4, 4, h_send, h_recv.at[three])
    forced_low(three)
    to_owners(lsnd, lbuf, 1, 1, b_send.at[1], b_recv.at[1])
    for c in ORDER:
        solved(c)
    for c in ORDER:
        placed(c)

    pltpu.make_async_copy(nb_s.at[pl.ds(0, 28)], nb_s.at[pl.ds(0, 28)], i_send.at[0]).wait()
    pltpu.make_async_copy(cnt_b.at[pl.ds(0, 7)], cnt_b.at[pl.ds(0, 7)], i_send.at[1]).wait()
    for sent, sem in (
        (vr.at[:, pl.ds(0, MODES - BAND)], a_send),
        (strs.at[pl.ds(0, NREAL - 1)], st_send),
        (snd.at[:, pl.ds(0, 210), :], h_send),
        (fsnd.at[pl.ds(0, 63), :], b_send.at[0]),
        (lsnd.at[pl.ds(0, 63), :], b_send.at[1]),
        (wsnd.at[:, pl.ds(0, 252), :], c_send),
    ):
        pltpu.make_async_copy(sent, sent, sem).wait()


def local(velocity, low_index, neighbours, owner_map, mode_counts, helmholtz):
    table = jnp.asarray(forward_table())
    hbm = pl.BlockSpec(memory_space=pl.ANY)
    vmem = pl.BlockSpec(memory_space=pltpu.VMEM)
    dma = pltpu.SemaphoreType.DMA
    held = pl.pallas_call(
        kernel,
        out_shape=pltpu.VMEM(velocity.shape, F32),
        in_specs=[hbm] * 7,
        out_specs=vmem,
        scratch_shapes=[
            pltpu.VMEM((COMP, MODES, 8, COLS), F32),
            pltpu.VMEM((COMP, MODES, 8, COLS), F32),
            pltpu.VMEM((COMP, MODES, 8, POINTS), F32),
            pltpu.VMEM((HIGH, 8, POINTS), F32),
            pltpu.VMEM((COMP, HIGH, 8, COLS), F32),
            pltpu.VMEM((MODES * 8, COLS), F32),
            pltpu.VMEM((COMP, 256, 128), F32),
            pltpu.VMEM((COMP, 256, 128), F32),
            pltpu.VMEM((SLOTS, 128), F32),
            pltpu.VMEM((SLOTS, 128), F32),
            pltpu.VMEM((SLOTS, 128), F32),
            pltpu.VMEM((SLOTS, 128), F32),
            pltpu.VMEM((COMP, 256, 128), F32),
            pltpu.VMEM((COMP, 256, 128), F32),
            pltpu.VMEM((NREAL, COMP, LOW * 8, COLS), F32),
            pltpu.VMEM((128, COLS), F32),
            pltpu.VMEM((128, 2 * COLS), BF16),
            pltpu.VMEM((COLS, 256), BF16),
            pltpu.VMEM((2 * MODES, 128), F32),
            pltpu.VMEM((2 * MODES, 2 * MODES), BF16),
            pltpu.VMEM((HEIGHTS, HEIGHTS), F32),
            pltpu.VMEM((4, HEIGHTS, 128), F32),
            pltpu.VMEM((HEIGHTS, HEIGHTS), BF16),
            pltpu.VMEM((HEIGHTS, HEIGHTS), BF16),
            pltpu.VMEM((3, COLS, POINTS), BF16),
            pltpu.VMEM((POINTS, 2 * COLS), BF16),
            pltpu.SMEM((MODES, LOW), jnp.int32),
            pltpu.SMEM((NKX, BAND), jnp.int32),
            pltpu.SMEM((MODES,), jnp.int32),
            pltpu.SMEM((MODES,), jnp.int32),
            pltpu.SMEM((LOW,), jnp.int32),
            pltpu.SMEM((SLOTS,), jnp.int32),
            dma,
            dma((COMP,)),
            dma((2,)),
            dma((2,)),
            dma,
            dma((COMP,)),
            dma,
            dma((COMP,)),
            dma((2,)),
            dma((2,)),
            dma,
            dma((COMP,)),
            dma((4,)),
        ],
        compiler_params=pltpu.CompilerParams(collective_id=0, has_side_effects=True),
    )(velocity, low_index, neighbours, owner_map, mode_counts, helmholtz, table)
    return held


def solution(mesh):
    in_specs = (
        P(None, "real", "kx", "ht", None),
        P(),
        P("kx", None),
        P(),
        P("kx"),
        P(("kx", "ht"), None, None),
    )
    out_specs = P(None, "real", "kx", "ht", None)
    return jax.shard_map(local, mesh=mesh, in_specs=in_specs, out_specs=out_specs, check_vma=False)
```

```python
import functools

import jax
import jax.numpy as jnp
import numpy as np
from jax import lax
from jax.experimental import pallas as pl
from jax.experimental.pallas import tpu as pltpu
from jax.sharding import PartitionSpec as P

MESH = pl.DeviceIdType.MESH
F32 = jnp.float32
BF16 = jnp.bfloat16

dt_step = 0.1


def ring(step, count):
    return min(step, count - step)


COMP, BAND, ROWS, COLS = 3, 4, 64, 128
NKX, NHT, NREAL = 8, 8, 4
MODES, LOW, POINTS, HEIGHTS, SLOTS = 32, 8, 256, 512, 64
HIGH = MODES - LOW
ORDER = (1, 0, 2)
FAR_FIRST = (4, 3, 5, 2, 6, 1, 7)
PAIRS = [(dk, dh) for dk in range(NKX) for dh in range(NHT) if dk + dh]
PAIRS.sort(key=lambda p: (-ring(p[1] // 2, NHT // 2), -ring(p[0], NKX)))


def forward_table():
    ids = np.arange(COLS)
    wave = (ids // 2).astype(np.float32)
    spots = np.float32(2.0 * np.pi) * np.arange(POINTS).astype(np.float32) / np.float32(POINTS)
    phases = (wave[:, None] * spots[None, :]).astype(np.float64)
    forward = (np.where(ids[:, None] % 2 == 0, np.cos(phases), -np.sin(phases)) / 8.0).astype(np.float32)
    head = forward.astype(BF16)
    return np.stack([head, head, (forward - head.astype(np.float32)).astype(BF16)])


def split(x):
    head = x.astype(BF16)
    return head, (x - head.astype(F32)).astype(BF16)


def mm(a, b):
    return lax.dot_general(a, b, (((1,), (0,)), ((), ())), preferred_element_type=F32)


def mm_nt(a, b):
    return lax.dot_general(a, b, (((1,), (1,)), ((), ())), preferred_element_type=F32)


def apply_forward(x, table):
    hi, lo = split(x)
    heads = table[pl.ds(0, 2)].reshape(2 * COLS, POINTS)
    return mm(jnp.concatenate([hi, lo], axis=1), heads) + mm(hi, table[2])


def apply_backward(x, both):
    hi, lo = split(x)
    part = mm(hi, both[...])
    return part[:, :COLS] + (part[:, COLS:] + mm(lo, both[:, :COLS]))


def kernel(
    v, low_h, nb_own, omap_h, cnt_own, helm, table,
    out,
    vr, cur, phys, hl, nl, upd, snd, ubuf, lsnd, lbuf, fsnd, fbuf, wsnd, rbuf, strs, onehot, oh, oht, order, om, hf, ht32, hth, htl,
    ft, back_t, nb_s, cnt_b, cnt_s, perm_s, low_s, omap_s,
    a_send, a_recv, i_send, i_recv, st_send, st_recv, h_send, h_recv, b_send, b_recv, c_send, c_recv, l_sem,
):
    kx, ht, re = lax.axis_index("kx"), lax.axis_index("ht"), lax.axis_index("real")
    kxs = [lax.rem(kx + d, NKX) for d in range(NKX)]
    hts = [lax.rem(ht + d, NHT) for d in range(NHT)]

    barrier = pltpu.get_barrier_semaphore()
    for d in FAR_FIRST:
        pl.semaphore_signal(barrier, 1, device_id=(kxs[d], ht, re), device_id_type=MESH)
    for d in FAR_FIRST:
        pl.semaphore_signal(barrier, 1, device_id=(kx, hts[d], re), device_id_type=MESH)
    for d in (2, 1, 3):
        pl.semaphore_signal(barrier, 1, device_id=(kx, ht, lax.rem(re + d, NREAL)), device_id_type=MESH)
    slot = kx * NHT + ht
    source = ht * NKX + kx
    pl.semaphore_wait(barrier, (NKX - 1) + (NHT - 1) + (NREAL - 1))

    def gather(c):
        for d in FAR_FIRST:
            pltpu.make_async_remote_copy(
                v.at[c, 0, :, pl.ds(kxs[d] * 8, 8), :],
                vr.at[c, pl.ds(kx * BAND, BAND)],
                a_send,
                a_recv.at[c],
                device_id=(kxs[d], ht, re),
                device_id_type=MESH,
            ).start()

    for d in FAR_FIRST:
        for own, held, i in ((nb_own, nb_s.at[pl.ds(kx * BAND, BAND)], 0), (cnt_own, cnt_b.at[kx], 1)):
            pltpu.make_async_remote_copy(
                own, held, i_send.at[i], i_recv.at[i], device_id=(kxs[d], ht, re), device_id_type=MESH
            ).start()
    gather(ORDER[0])
    for c in ORDER[1:]:
        gather(c)
    local = [
        pltpu.make_async_copy(src, dst, l_sem.at[i])
        for i, (src, dst) in enumerate(((low_h, low_s), (omap_h, omap_s), (table, ft), (helm.at[0], hf)))
    ]
    for copy in local:
        copy.start()
    for c in ORDER:
        pltpu.make_async_copy(
            v.at[c, 0, :, pl.ds(kx * 8, 8), :], vr.at[c, pl.ds(kx * BAND, BAND)], a_recv.at[c]
        ).start()
    pltpu.make_async_copy(nb_own, nb_s.at[pl.ds(kx * BAND, BAND)], i_recv.at[0]).start()
    pltpu.make_async_copy(cnt_own, cnt_b.at[kx], i_recv.at[1]).start()
    for copy in local:
        copy.wait()

    lane = lax.broadcasted_iota(jnp.int32, (1, COLS), 1)

    def one_row(s, _):
        for p in range(2):
            onehot[pl.ds(p * SLOTS + s, 1), :] = (lane == 2 * omap_s[s] + p).astype(F32)
        return 0

    lax.fori_loop(0, SLOTS, one_row, 0)
    square = onehot[...]
    turn = square.T
    for i in range(2):
        oh[:, pl.ds(i * 128, 128)] = square.astype(BF16)
        oht[:, pl.ds(i * 128, 128)] = turn.astype(BF16)

    lows = [low_s[j] for j in range(LOW)]
    ranked = list(lows)
    for i in range(LOW):
        for j in range(i % 2, LOW - 1, 2):
            one, two = ranked[j], ranked[j + 1]
            ranked[j], ranked[j + 1] = jnp.minimum(one, two), jnp.maximum(one, two)

    def one_high(q, _):
        mode = q
        for low in ranked:
            mode = mode + (low <= mode).astype(jnp.int32)
        perm_s[q] = mode
        return 0

    lax.fori_loop(0, HIGH, one_high, 0)
    for j in range(LOW):
        perm_s[HIGH + j] = lows[j]

    def one_mode(m, _):
        place = m
        for low in lows:
            place = place - (low < m).astype(jnp.int32)
        for j, low in enumerate(lows):
            place = jnp.where(low == m, jnp.int32(HIGH + j), place)
        order[pl.ds(m, 1), :] = (lane == place).astype(F32)
        order[pl.ds(MODES + m, 1), :] = (lane == MODES + place).astype(F32)
        return 0

    lax.fori_loop(0, MODES, one_mode, 0)
    om[...] = order[:, : 2 * MODES].astype(BF16)
    back_t[:, pl.ds(0, COLS)] = (ft[0].astype(F32).T * 0.5).astype(BF16)
    back_t[:, pl.ds(COLS, COLS)] = (ft[2].astype(F32).T * 0.5).astype(BF16)
    for i in range(4):
        for j in range(4):
            ht32[i, pl.ds(j * 128, 128), :] = hf[pl.ds(i * 128, 128), pl.ds(j * 128, 128)].T
    for y in range(4):
        for a in range(2):
            for i in range(4):
                rows = [ht32[i, pl.ds(h * 64 + a * 4 + y, NKX, stride=8), :] for h in range(NHT)]
                head, tail = split(jnp.concatenate(rows, axis=0))
                hth[pl.ds((y * 2 + a) * 64, 64), pl.ds(i * 128, 128)] = head
                htl[pl.ds((y * 2 + a) * 64, 64), pl.ds(i * 128, 128)] = tail
    pltpu.make_async_copy(nb_s, nb_s, i_recv.at[0]).wait()
    pltpu.make_async_copy(cnt_b, cnt_b, i_recv.at[1]).wait()
    for m in range(MODES):
        cnt_s[m] = cnt_b[m // BAND, m % BAND]

    def products(c):
        pltpu.make_async_copy(vr.at[c], vr.at[c], a_recv.at[c]).wait()
        fields = vr[c].reshape(MODES * 8, COLS)
        cur[c] = vr[c]
        phys[c] = apply_forward(fields, ft).reshape(MODES, 8, POINTS)
        def stress_band(band, sums):
            sums = list(sums)
            for row in range(BAND):
                mode = perm_s[band * BAND + row]
                mine = phys[c, mode]
                for j in range(LOW):
                    sums[j] = sums[j] + mine * phys[1, nb_s[mode, j]]
            return tuple(sums)

        zeros = tuple(jnp.zeros((8, POINTS), F32) for _ in range(LOW))
        stress = jnp.concatenate(lax.fori_loop(0, HIGH // BAND, stress_band, zeros), axis=0)
        here = strs.at[re, c]
        here[...] = apply_backward(stress * (1.0 / NREAL), back_t)
        for d in (2, 1, 3):
            pltpu.make_async_remote_copy(
                here,
                here,
                st_send,
                st_recv.at[c],
                device_id=(kx, ht, lax.rem(re + d, NREAL)),
                device_id_type=MESH,
            ).start()
        low_1 = [phys[1, low_s[j]] for j in range(LOW)]
        low_c = low_1 if c == 1 else [phys[c, low_s[j]] for j in range(LOW)]

        def high_band(band, _):
            for row in range(BAND):
                mode = perm_s[band * BAND + row]
                first, second = [], []
                for j in range(LOW):
                    near = nb_s[mode, j]
                    first.append(low_c[j] * phys[1, near])
                    if c != 1:
                        second.append(low_1[j] * phys[c, near])
                total = functools.reduce(lambda a, b: a + b, first)
                total = total + (total if c == 1 else functools.reduce(lambda a, b: a + b, second))
                hl[band * BAND + row] = total
            return 0

        lax.fori_loop(0, HIGH // BAND, high_band, 0)
        nl[c] = apply_backward(hl[...].reshape(HIGH * 8, POINTS), back_t).reshape(HIGH, 8, COLS)

    half_lane = lax.broadcasted_iota(jnp.int32, (8, COLS), 1) // 2
    odd = (lax.broadcasted_iota(jnp.int32, (SLOTS, 128), 1) // 32) % 2 == 1

    def gain(mode):
        return jnp.where(half_lane < cnt_s[mode], F32(dt_step), F32(0.0))

    def turned(tiles):
        rows = [
            upd[pl.ds(group * 64 + a * 4 + y, 8, stride=8), :]
            for pair in tiles
            for a in range(2)
            for group in pair
            for y in range(4)
        ]
        hi, lo = split(jnp.concatenate(rows, axis=0))
        both = mm_nt(oh[...], jnp.concatenate([hi, lo], axis=1))
        given = []
        for tile in range(len(tiles)):
            even_p = both[:SLOTS, tile * 128 : tile * 128 + 128]
            odd_p = both[SLOTS:, tile * 128 : tile * 128 + 128]
            given.append(jnp.where(odd, pltpu.roll(odd_p, 32, 1), even_p))
            given.append(jnp.where(odd, odd_p, pltpu.roll(even_p, 96, 1)))
        return given

    def to_owners(given, taken, stride, count, send, recv):
        pltpu.make_async_copy(
            given.at[pl.ds(slot * stride, count), :], taken.at[pl.ds(source * stride, count), :], recv
        ).start()
        for dk, dh in PAIRS:
            to_kx, to_ht = kxs[dk], hts[dh]
            pltpu.make_async_remote_copy(
                given.at[pl.ds((to_kx * NHT + to_ht) * stride, count), :],
                taken.at[pl.ds(source * stride, count), :],
                send,
                recv,
                device_id=(to_kx, to_ht, re),
                device_id_type=MESH,
            ).start()

    def forced_high(c):
        def one_band(band, _):
            for row in range(BAND):
                q = band * BAND + row
                mode = perm_s[q]
                upd[pl.ds(q * 8, 8), :] = cur[c, mode] + gain(mode) * nl[c, q]
            return 0

        lax.fori_loop(0, HIGH // BAND, one_band, 0)
        for group, value in enumerate(turned(((0, 1), (2, 2)))[:3]):
            snd[c, pl.ds(group, SLOTS, stride=4), :] = value

    def forced_low(c):
        pltpu.make_async_copy(strs.at[pl.ds(0, 3), 0], strs.at[pl.ds(0, 3), 0], st_recv.at[c]).wait()
        summed = (strs[0, c] + strs[1, c]) + (strs[2, c] + strs[3, c])
        for j in range(LOW):
            mode = low_s[j]
            upd[pl.ds((HIGH + j) * 8, 8), :] = cur[c, mode] + gain(mode) * summed[j * 8 : j * 8 + 8]
        value = turned(((3, 3),))[0]
        if c == ORDER[2]:
            lsnd[...] = value
        elif c == ORDER[0]:
            fsnd[...] = value
        else:
            snd[ORDER[ORDER.index(c) + 1], pl.ds(3, SLOTS, stride=4), :] = value

    first_half = lax.broadcasted_iota(jnp.int32, (MODES, 128), 1) < 64

    def solved(c):
        place = ORDER.index(c)
        if place == 0:
            arrived = ubuf.at[c, pl.ds(0, 3 * SLOTS), :]
            pltpu.make_async_copy(arrived, arrived, h_recv.at[c]).wait()
            pltpu.make_async_copy(fbuf, fbuf, b_recv.at[0]).wait()
        elif place == 1:
            arrived = ubuf.at[c, pl.ds(0, 3 * SLOTS), :]
            pltpu.make_async_copy(arrived, arrived, h_recv.at[c]).wait()
            pltpu.make_async_copy(ubuf.at[ORDER[2]], ubuf.at[ORDER[2]], h_recv.at[ORDER[2]]).wait()
        else:
            pltpu.make_async_copy(lbuf, lbuf, b_recv.at[1]).wait()
        groups = []
        for group in range(4):
            if group < 3:
                given = ubuf[c, pl.ds(group, SLOTS, stride=4), :]
            else:
                low = (fbuf, None, lbuf)[place]
                given = ubuf[ORDER[2], pl.ds(3, SLOTS, stride=4), :] if place == 1 else low[...]
            groups.append(jnp.concatenate([given, pltpu.roll(given, 64, 1)], axis=0).T[:64])
        fields = jnp.concatenate(
            [
                jnp.concatenate([groups[g][(p * 4 + y) * 8 : (p * 4 + y) * 8 + 8] for y in range(4)], axis=1)
                for p in range(2)
                for g in range(4)
            ],
            axis=0,
        )
        hi, lo = split(fields)
        hi = mm(om[...], hi).astype(BF16)
        lo = mm(om[...], lo).astype(BF16)
        part = mm(jnp.concatenate([hi, lo], axis=0), hth[...])
        answer = part[: 2 * MODES] + (mm(hi, htl[...]) + part[2 * MODES :])
        for tile in range(4):
            even_p = answer[:MODES, tile * 128 : tile * 128 + 128]
            odd_p = answer[MODES:, tile * 128 : tile * 128 + 128]
            wsnd[c, pl.ds((2 * tile) * MODES, MODES), :] = jnp.where(
                first_half, even_p, pltpu.roll(odd_p, 64, 1)
            )
            wsnd[c, pl.ds((2 * tile + 1) * MODES, MODES), :] = jnp.where(
                first_half, pltpu.roll(even_p, 64, 1), odd_p
            )
        pltpu.make_async_copy(
            wsnd.at[c, pl.ds(ht * MODES + kx * 4, 4), :], rbuf.at[c, pl.ds(slot * 4, 4), :], c_recv.at[c]
        ).start()

        for dk, dh in PAIRS:
            to_kx, to_ht = kxs[dk], hts[dh]
            pltpu.make_async_remote_copy(
                wsnd.at[c, pl.ds(to_ht * MODES + to_kx * 4, 4), :],
                rbuf.at[c, pl.ds(slot * 4, 4), :],
                c_send,
                c_recv.at[c],
                device_id=(to_kx, to_ht, re),
                device_id_type=MESH,
            ).start()

    def placed(c):
        pltpu.make_async_copy(rbuf.at[c], rbuf.at[c], c_recv.at[c]).wait()
        low_half = lax.broadcasted_iota(jnp.int32, (SLOTS, 128), 1) < 64
        columns = []
        for pair in range(2):
            one = rbuf[c, pl.ds(2 * pair, SLOTS, stride=4), :]
            two = rbuf[c, pl.ds(2 * pair + 1, SLOTS, stride=4), :]
            columns.append(
                jnp.concatenate(
                    [
                        jnp.where(low_half, one, pltpu.roll(two, 64, 1)),
                        jnp.where(low_half, pltpu.roll(one, 64, 1), two),
                    ],
                    axis=0,
                )
            )
        hi, lo = split(jnp.concatenate(columns, axis=1))
        back = mm(oht[...], jnp.concatenate([hi, lo], axis=0))
        for pair in range(2):
            out[c, 0, pl.ds(2 * pair, 2), :, :] = back[:, pair * 128 : pair * 128 + 128].T.reshape(2, ROWS, COLS)

    one, two, three = ORDER
    products(one)
    forced_high(one)
    to_owners(snd.at[one], ubuf.at[one], 4, 3, h_send, h_recv.at[one])
    products(two)
    forced_high(two)
    to_owners(snd.at[two], ubuf.at[two], 4, 3, h_send, h_recv.at[two])
    forced_low(one)
    to_owners(fsnd, fbuf, 1, 1, b_send.at[0], b_recv.at[0])
    products(three)
    forced_high(three)
    forced_low(two)
    to_owners(snd.at[three], ubuf.at[three], 4, 4, h_send, h_recv.at[three])
    forced_low(three)
    to_owners(lsnd, lbuf, 1, 1, b_send.at[1], b_recv.at[1])
    for c in ORDER:
        solved(c)
    for c in ORDER:
        placed(c)

    pltpu.make_async_copy(nb_s.at[pl.ds(0, 28)], nb_s.at[pl.ds(0, 28)], i_send.at[0]).wait()
    pltpu.make_async_copy(cnt_b.at[pl.ds(0, 7)], cnt_b.at[pl.ds(0, 7)], i_send.at[1]).wait()
    for sent, sem in (
        (vr.at[:, pl.ds(0, MODES - BAND)], a_send),
        (strs.at[pl.ds(0, NREAL - 1)], st_send),
        (snd.at[:, pl.ds(0, 210), :], h_send),
        (fsnd.at[pl.ds(0, 63), :], b_send.at[0]),
        (lsnd.at[pl.ds(0, 63), :], b_send.at[1]),
        (wsnd.at[:, pl.ds(0, 252), :], c_send),
    ):
        pltpu.make_async_copy(sent, sent, sem).wait()


def local(velocity, low_index, neighbours, owner_map, mode_counts, helmholtz):
    table = jnp.asarray(forward_table())
    hbm = pl.BlockSpec(memory_space=pl.ANY)
    vmem = pl.BlockSpec(memory_space=pltpu.VMEM)
    dma = pltpu.SemaphoreType.DMA
    held = pl.pallas_call(
        kernel,
        out_shape=pltpu.VMEM(velocity.shape, F32),
        in_specs=[hbm] * 7,
        out_specs=vmem,
        scratch_shapes=[
            pltpu.VMEM((COMP, MODES, 8, COLS), F32),
            pltpu.VMEM((COMP, MODES, 8, COLS), F32),
            pltpu.VMEM((COMP, MODES, 8, POINTS), F32),
            pltpu.VMEM((HIGH, 8, POINTS), F32),
            pltpu.VMEM((COMP, HIGH, 8, COLS), F32),
            pltpu.VMEM((MODES * 8, COLS), F32),
            pltpu.VMEM((COMP, 256, 128), F32),
            pltpu.VMEM((COMP, 256, 128), F32),
            pltpu.VMEM((SLOTS, 128), F32),
            pltpu.VMEM((SLOTS, 128), F32),
            pltpu.VMEM((SLOTS, 128), F32),
            pltpu.VMEM((SLOTS, 128), F32),
            pltpu.VMEM((COMP, 256, 128), F32),
            pltpu.VMEM((COMP, 256, 128), F32),
            pltpu.VMEM((NREAL, COMP, LOW * 8, COLS), F32),
            pltpu.VMEM((128, COLS), F32),
            pltpu.VMEM((128, 2 * COLS), BF16),
            pltpu.VMEM((COLS, 256), BF16),
            pltpu.VMEM((2 * MODES, 128), F32),
            pltpu.VMEM((2 * MODES, 2 * MODES), BF16),
            pltpu.VMEM((HEIGHTS, HEIGHTS), F32),
            pltpu.VMEM((4, HEIGHTS, 128), F32),
            pltpu.VMEM((HEIGHTS, HEIGHTS), BF16),
            pltpu.VMEM((HEIGHTS, HEIGHTS), BF16),
            pltpu.VMEM((3, COLS, POINTS), BF16),
            pltpu.VMEM((POINTS, 2 * COLS), BF16),
            pltpu.SMEM((MODES, LOW), jnp.int32),
            pltpu.SMEM((NKX, BAND), jnp.int32),
            pltpu.SMEM((MODES,), jnp.int32),
            pltpu.SMEM((MODES,), jnp.int32),
            pltpu.SMEM((LOW,), jnp.int32),
            pltpu.SMEM((SLOTS,), jnp.int32),
            dma,
            dma((COMP,)),
            dma((2,)),
            dma((2,)),
            dma,
            dma((COMP,)),
            dma,
            dma((COMP,)),
            dma((2,)),
            dma((2,)),
            dma,
            dma((COMP,)),
            dma((4,)),
        ],
        compiler_params=pltpu.CompilerParams(collective_id=0, has_side_effects=True),
    )(velocity, low_index, neighbours, owner_map, mode_counts, helmholtz, table)
    return held


def solution(mesh):
    in_specs = (
        P(None, "real", "kx", "ht", None),
        P(),
        P("kx", None),
        P(),
        P("kx"),
        P(("kx", "ht"), None, None),
    )
    out_specs = P(None, "real", "kx", "ht", None)
    return jax.shard_map(local, mesh=mesh, in_specs=in_specs, out_specs=out_specs, check_vma=False)
```
